256 devices in a mesh: strip: 64 (over y, z_lo, x), group: 4 (over z_hi, core).
Axes of the slice: x: 4, y: 4, z: 8 (z_hi: 2, z_lo: 4; z = z_hi * 4 + z_lo), core: 2. Of those that a mesh axis runs over, the one named last changes fastest.
Arguments:
- initial: float32 [64, 256, 128], P('group', 'strip'), may hold values from -1 to 1
- react_rates: float32 [64], P('group'), may hold values from 0.02 to 0.1
- snap_times: int32 [64, 4], replicated, may hold values from 1 to 2
- field_code: bfloat16 [64, 512], replicated, may hold values from -6 to 6
- time_code: bfloat16 [2, 512], replicated, may hold values from -6 to 6
- batch_ids: int32 [2, 512], P(None, 'group'), may hold values from 0 to 63
- in_weight: bfloat16 [512, 512], replicated, may hold values from -0.25 to 0.25
- in_moment: float32 [512, 512], P('strip'), may hold values from -0.75 to 0.75
- in_second: float32 [512, 512], P('strip'), may hold values from 0.001 to 0.1
- out_weight: bfloat16 [512, 32768], P(None, 'strip'), may hold values from -0.75 to 0.75
- out_moment: float32 [512, 32768], P('group', 'strip'), may hold values from -0.0625 to 0.0625
- out_second: float32 [512, 32768], P('group', 'strip'), may hold values from 1e-06 to 0.0001
Outputs:
- fields_out: float32 [64, 256, 128], P('group', 'strip')
- in_weight_new: bfloat16 [512, 512], replicated
- in_moment_new: float32 [512, 512], P('strip')
- in_second_new: float32 [512, 512], P('strip')
- out_weight_new: bfloat16 [512, 32768], P(None, 'strip')
- out_moment_new: float32 [512, 32768], P('group', 'strip')
- out_second_new: float32 [512, 32768], P('group', 'strip')
The draws below stay inside these ranges and needn't reach their ends.
Inputs may be any that keep to these rules, and one draw needn't show every extreme that they name: `snap_times`: the number of solver steps after which snapshot slot k of field f is taken. `batch_ids`: column c of a row names a sample of batch part c // 128: field id, slot c // 128.
All inputs are finite; a program needn't handle non-finite values.
Results may differ from the reference program's by a relative error of at most 0.001.
The reference program's roundings to bfloat16 on the way (of `snapshots`, `layout`, `inputs`, `target`, `hidden`, `delta_out` and `pre_grad`) count: a program that leaves them out, or rounds other values in their place, can miss the bound.
Values may be sent and summed in bfloat16 or wider, within the bound.
A program may use at most 64 MiB of HBM per device.

```python
import math
import jax
import jax.numpy as jnp

HID = 512
COLS = 128
MB = 128
STEPS = 2
SNAPS = 4
ADAM = 2
PRIOR = 100
FIELDS = 64
ROWS = 256
POINTS = 32768
PIECE = 8
SNAP_PART = 1
POOL = 64
BATCH = 512
N_STRIP = 64


def plant(entries, own_key, low, top_value):
    extent = entries.shape
    index_at = [jax.random.randint(jax.random.fold_in(own_key, axis), (), 0, extent[axis]) for axis in range(len(extent))]
    entries = entries.at[tuple(index_at)].set(low)
    longest = extent.index(max(extent))
    index_at[longest] = (index_at[longest] + 1) % extent[longest]
    return entries.at[tuple(index_at)].set(top_value)


def strengthened(drawn, own_key, source, target, shards_of, factor):
    def block_of(position):
        return (jnp.arange(drawn.shape[position]) // (drawn.shape[position] // shards_of)).reshape((-1,) + (1,) * (drawn.ndim - 1 - position))

    one_side = jax.random.permutation(own_key, shards_of)[block_of(target)]
    far = (block_of(target) + shards_of // 2) % shards_of
    return jnp.where((block_of(source) == one_side) | (block_of(source) == far), factor * drawn, drawn)


def steps_of(rng, extent, cuts, smallest, top_value):
    gain = 1.0
    for axis_at, parts in cuts:
        steps = jax.random.uniform(jax.random.fold_in(jax.random.fold_in(rng, 6), axis_at), (parts,), jnp.float32, smallest / len(cuts), top_value / len(cuts))
        gain = gain * jnp.repeat(jnp.exp(steps), extent[axis_at] // parts).reshape((-1,) + (1,) * (len(extent) - 1 - axis_at))
    return gain


def normal_values(own_key, extent, width, bound, shards=(), kind=jnp.bfloat16):
    gain = steps_of(own_key, extent, shards, -0.22, 0.18) if shards else 1.0
    values = jax.random.normal(own_key, extent, jnp.float32) * width * gain
    return jnp.minimum(jnp.maximum(values, -bound), bound).astype(kind)


def heavy_noise(key, dims, width, most, split, heavy, kind=jnp.bfloat16):
    result = width * jax.random.normal(key, dims, jnp.float32)
    if split:
        result = result * steps_of(key, dims, split, -0.22, 0.18)
    return jnp.clip(strengthened(result, jax.random.fold_in(key, 3), *heavy), -most, most).astype(kind)


def setup_inputs(seed: int = 0) -> dict:
    splits = jax.random.split(jax.random.key(seed), 13)
    initial = jnp.clip(jax.random.uniform(splits[0], (FIELDS, ROWS, COLS), jnp.float32, -1.0, 1.0) * steps_of(splits[0], (FIELDS, ROWS, COLS), ((0, 4), (1, 64)), -0.4, 0.0), -1.0, 1.0)
    react_rates = jnp.clip(jnp.exp(math.log(0.1) - 1.609438 * jax.random.uniform(splits[1], (FIELDS,), jnp.float32) ** steps_of(splits[1], (FIELDS,), ((0, 4),), -0.2, 0.2)), 0.02, 0.1)
    snap_times = plant(jax.random.randint(splits[2], (FIELDS, SNAPS), 1, STEPS + 1), jax.random.fold_in(splits[2], 1), 1, STEPS).astype(jnp.int32)
    field_code = normal_values(splits[3], (FIELDS, HID), 1.0, 6.0)
    time_code = normal_values(splits[4], (STEPS, HID), 1.0, 6.0)
    batch_ids = plant(jax.random.randint(splits[5], (ADAM, BATCH), 0, POOL), jax.random.fold_in(splits[5], 1), 0, POOL - 1).astype(jnp.int32)
    in_weight = normal_values(splits[6], (HID, HID), HID ** -0.5, 0.25)
    in_moment = normal_values(splits[7], (HID, HID), 0.05, 0.75, ((0, 64),), jnp.float32)
    in_second = jnp.clip(jnp.exp(math.log(0.1) - 4.6051702 * jax.random.uniform(splits[8], (HID, HID), jnp.float32) ** steps_of(splits[8], (HID, HID), ((0, 64),), -0.2, 0.2)), 0.001, 0.1)
    out_weight = heavy_noise(splits[9], (HID, POINTS), HID ** -0.5, 0.75, ((1, 64),), (1, 0, 64, 4.0))
    out_moment = normal_values(splits[10], (HID, POINTS), 0.004, 0.0625, ((0, 4), (1, 64)), jnp.float32)
    out_second = jnp.clip(jnp.exp(math.log(0.0001) - 4.6051702 * jax.random.uniform(splits[11], (HID, POINTS), jnp.float32) ** steps_of(splits[11], (HID, POINTS), ((0, 4), (1, 64)), -0.2, 0.2)), 9.999999974752427e-07, 0.0001)
    return {"initial": initial, "react_rates": react_rates, "snap_times": snap_times, "field_code": field_code, "time_code": time_code, "batch_ids": batch_ids, "in_weight": in_weight, "in_moment": in_moment, "in_second": in_second, "out_weight": out_weight, "out_moment": out_moment, "out_second": out_second}


DIFF_ROWS = 0.35
DIFF_COLS = 0.05
BETA_ONE = 0.9
BETA_TWO = 0.999
LEARN_RATE = 0.003
EPSILON = 1e-08
GELU_SCALE = 0.7978845608
GELU_CUBE = 0.044715

def advance(padded, react_rates):
    center = padded[:, 1:-1]
    across = jnp.roll(center, 1, 2) + jnp.roll(center, -1, 2)
    return center + DIFF_ROWS * (padded[:, :-2] + padded[:, 2:] - 2.0 * center) + DIFF_COLS * (across - 2.0 * center) + react_rates[:, None, None] * center * (1.0 - center * center)

def gelu_value(pre_act):
    return 0.5 * pre_act * (1.0 + jnp.tanh(GELU_SCALE * (pre_act + GELU_CUBE * pre_act * pre_act * pre_act)))

def gelu_slope(pre_act):
    tanh_part = jnp.tanh(GELU_SCALE * (pre_act + GELU_CUBE * pre_act * pre_act * pre_act))
    return 0.5 * (1.0 + tanh_part) + 0.5 * pre_act * (1.0 - tanh_part * tanh_part) * GELU_SCALE * (1.0 + 3.0 * GELU_CUBE * pre_act * pre_act)

def adam_update(weight, moment, second, gradient, step_count):
    moment = BETA_ONE * moment + (1.0 - BETA_ONE) * gradient
    second = BETA_TWO * second + (1.0 - BETA_TWO) * gradient * gradient
    update = moment / (1.0 - BETA_ONE ** step_count) / (jnp.sqrt(second / (1.0 - BETA_TWO ** step_count)) + EPSILON)
    return ((weight.astype(jnp.float32) - LEARN_RATE * update).astype(jnp.bfloat16), moment, second)

def reference(initial, react_rates, snap_times, field_code, time_code, batch_ids, in_weight, in_moment, in_second, out_weight, out_moment, out_second):
    field_count = initial.shape[0]
    field_state = initial
    snapshots = jnp.zeros((field_count, SNAPS, ROWS, COLS), jnp.bfloat16)
    for solver_step in range(STEPS):
        field_state = advance(jnp.pad(field_state, ((0, 0), (1, 1), (0, 0))), react_rates)
        chosen = (snap_times == solver_step + 1)[:, :, None, None]
        snapshots = jnp.where(chosen, field_state.astype(jnp.bfloat16)[:, None], snapshots)
    layout = snapshots.reshape(field_count, SNAPS, N_STRIP, N_STRIP, PIECE)
    layout = jnp.transpose(layout, (0, 1, 3, 2, 4)).reshape(field_count * SNAPS, POINTS)
    column = jnp.arange(BATCH, dtype=jnp.int32)
    batch_part = column // MB
    for adam_turn in range(ADAM):
        sample_ids = batch_ids[adam_turn]
        field_of = sample_ids // SNAP_PART
        slot_of = batch_part * SNAP_PART + sample_ids % SNAP_PART
        time_of = snap_times[field_of, slot_of]
        inputs = (field_code[field_of].astype(jnp.float32) + time_code[time_of - 1].astype(jnp.float32)).astype(jnp.bfloat16)
        target = layout[field_of * SNAPS + slot_of].astype(jnp.float32)
        pre_act = jnp.dot(inputs, in_weight.T, preferred_element_type=jnp.float32)
        hidden = gelu_value(pre_act).astype(jnp.bfloat16)
        predict = jnp.dot(hidden, out_weight, preferred_element_type=jnp.float32)
        delta_out = ((predict - target) / BATCH).astype(jnp.bfloat16)
        out_grad = jnp.dot(hidden.T, delta_out, preferred_element_type=jnp.float32)
        hidden_grad = jnp.dot(delta_out, out_weight.T, preferred_element_type=jnp.float32)
        pre_grad = (hidden_grad * gelu_slope(pre_act)).astype(jnp.bfloat16)
        in_grad = jnp.dot(pre_grad.T, inputs, preferred_element_type=jnp.float32)
        step_count = PRIOR + adam_turn + 1
        in_weight, in_moment, in_second = adam_update(in_weight, in_moment, in_second, in_grad, step_count)
        out_weight, out_moment, out_second = adam_update(out_weight, out_moment, out_second, out_grad, step_count)
    return (field_state, in_weight, in_moment, in_second, out_weight, out_moment, out_second)
```

```python
import functools

import jax
import jax.numpy as jnp
from jax import lax
from jax.experimental import pallas as pl
from jax.experimental.pallas import tpu as pltpu
from jax.sharding import PartitionSpec as P

STEPS = 2
SNAPS = 4
ADAM = 2
PRIOR = 100

DIFF_ROWS = 0.35
DIFF_COLS = 0.05
BETA_ONE = 0.9
BETA_TWO = 0.999
LEARN_RATE = 0.003
EPSILON = 1e-08
GELU_SCALE = 0.7978845608
GELU_CUBE = 0.044715

MESH = pl.DeviceIdType.MESH
F32 = jnp.float32
BF16 = jnp.bfloat16


def gelu_value(pre_act):
    return (
        0.5
        * pre_act
        * (1.0 + jnp.tanh(GELU_SCALE * (pre_act + GELU_CUBE * pre_act * pre_act * pre_act)))
    )


def gelu_slope(pre_act):
    tanh_part = jnp.tanh(GELU_SCALE * (pre_act + GELU_CUBE * pre_act * pre_act * pre_act))
    return 0.5 * (1.0 + tanh_part) + 0.5 * pre_act * (1.0 - tanh_part * tanh_part) * GELU_SCALE * (
        1.0 + 3.0 * GELU_CUBE * pre_act * pre_act
    )


def adam_update(weight, moment, second, gradient, step_count):
    moment = BETA_ONE * moment + (1.0 - BETA_ONE) * gradient
    second = BETA_TWO * second + (1.0 - BETA_TWO) * gradient * gradient
    update = (
        moment
        / (1.0 - BETA_ONE**step_count)
        / (jnp.sqrt(second / (1.0 - BETA_TWO**step_count)) + EPSILON)
    )
    return ((weight.astype(F32) - LEARN_RATE * update).astype(BF16), moment, second)


def dot(left, right, left_dim, right_dim):
    return lax.dot_general(
        left, right, (((left_dim,), (right_dim,)), ((), ())), preferred_element_type=F32
    )


def three_parts(value):
    high = value.astype(BF16)
    rest = value - high.astype(F32)
    middle = rest.astype(BF16)
    low = (rest - middle.astype(F32)).astype(BF16)
    return high, middle, low


def kernel(
    initial,
    rates,
    times,
    field_code,
    time_code,
    batch_ids,
    in_weight,
    in_moment,
    in_second,
    out_weight,
    out_moment,
    out_second,
    fields_out,
    in_weight_new,
    in_moment_new,
    in_second_new,
    out_weight_new,
    out_moment_new,
    out_second_new,
    edges,
    halo,
    states,
    pieces,
    from_own,
    from_far,
    half_pool,
    core_pool,
    counts,
    terms,
    term_in,
    hidden_own,
    hidden_all,
    rows_own,
    weight_mid,
    halo_send,
    halo_recv,
    piece_send,
    own_recv,
    far_recv,
    pool_send,
    pool_recv,
    count_send,
    count_recv,
    term_send,
    term_recv,
    hidden_send,
    hidden_recv,
    weight_send,
    weight_recv,
    row_send,
    row_recv,
):
    strips = lax.axis_size("strip")
    me = lax.axis_index("strip")
    g = lax.axis_index("group")
    far = lax.rem(g + 2, 4)
    mate = g + 1 - 2 * lax.rem(g, 2)
    far_mate = lax.rem(mate + 2, 4)
    fields = initial.shape[0]
    others = strips - 1

    def other(k):
        return lax.rem(me + 1 + k, strips)

    def send(source, target, send_sem, recv_sem, strip, group):
        copy = pltpu.make_async_remote_copy(
            src_ref=source,
            dst_ref=target,
            send_sem=send_sem,
            recv_sem=recv_sem,
            device_id={"strip": strip, "group": group},
            device_id_type=MESH,
        )
        copy.start()
        return copy

    barrier = pltpu.get_barrier_semaphore()

    def greet(strip, group):
        pl.semaphore_signal(
            barrier, inc=1, device_id={"strip": strip, "group": group}, device_id_type=MESH
        )

    def greet_strip(k, carry):
        greet(other(k), g)
        greet(other(k), far)
        return carry

    lax.fori_loop(0, others, greet_strip, 0)
    greet(me, far)
    greet(me, mate)
    greet(me, far_mate)

    edges[0] = initial[:, 0:2, :]
    edges[1] = initial[:, 2:4, :]

    kind_row = lax.broadcasted_iota(jnp.int32, (128, 128), 0)
    field_row = 16 * (kind_row // 32) + lax.rem(kind_row, 16)
    kind_lane = lax.broadcasted_iota(jnp.int32, (64, 128), 1)
    field_lane = 16 * (kind_lane // 32) + lax.rem(kind_lane, 16)
    spread = (lax.broadcasted_iota(jnp.int32, (64, 128), 0) == field_lane).astype(F32).astype(BF16)
    kind_times = dot(times[...].astype(F32).astype(BF16), spread, 1, 0)
    slot = lax.broadcasted_iota(jnp.int32, (4, 128), 0)
    own_time = jnp.sum(jnp.where(slot == g, kind_times, 0.0), axis=0, keepdims=True)
    step_lane = (lax.rem(lax.broadcasted_iota(jnp.int32, (1, 128), 1) // 16, 2) + 1).astype(F32)
    time_fits = jnp.where(own_time == step_lane, 1.0, 0.0)
    ones = jnp.ones((8, 128), BF16)
    for turn in range(ADAM):
        hits = (batch_ids[turn : turn + 1, :] == field_row).astype(F32).astype(BF16)
        counts[0, turn] = dot(ones, hits, 1, 1) * time_fits

    pl.semaphore_wait(barrier, 2 * others + 3)

    up = lax.rem(me + others, strips)
    down = lax.rem(me + 1, strips)
    halo_copies = [
        send(edges.at[0], halo.at[1], halo_send.at[0], halo_recv.at[1], up, g),
        send(edges.at[1], halo.at[0], halo_send.at[1], halo_recv.at[0], down, g),
    ]
    count_copies = [
        send(counts.at[0], counts.at[1 + i], count_send.at[i], count_recv.at[i], me, group)
        for i, group in enumerate((far, mate, far_mate))
    ]

    code_parts = []
    for part in range(4):
        for step in range(STEPS):
            code_parts.append(
                (
                    field_code[16 * part : 16 * part + 16, :].astype(F32)
                    + time_code[step : step + 1, :].astype(F32)
                ).astype(BF16)
            )
    code = jnp.concatenate(code_parts, axis=0)
    hidden_width = 8 * strips
    pre_act = dot(in_weight[...].reshape(hidden_width, 512), code, 1, 1)
    hidden = gelu_value(pre_act).astype(BF16)
    hidden_all[0] = hidden.reshape(strips, 8, 128)
    old_weight = out_weight[...].reshape(hidden_width, 512)
    predict = dot(hidden, old_weight, 0, 0)
    own_pre = dot(in_weight[me], code, 1, 1)

    for copy in halo_copies:
        copy.wait()

    row = lax.broadcasted_iota(jnp.int32, (8, 128), 0) + 4 * me - 2
    inside = jnp.logical_and(row >= 0, row < 4 * strips)

    def advance(center, rate):
        across = pltpu.roll(center, 1, 1) + pltpu.roll(center, 127, 1)
        return (
            center
            + DIFF_ROWS * (pltpu.roll(center, 1, 0) + pltpu.roll(center, 7, 0) - 2.0 * center)
            + DIFF_COLS * (across - 2.0 * center)
            + rate * center * (1.0 - center * center)
        )

    for field in range(fields):
        start = jnp.concatenate([halo[0, field], initial[field], halo[1, field]], axis=0)
        start = jnp.where(inside, start, 0.0)
        first = jnp.where(inside, advance(start, rates[field]), 0.0)
        second = advance(first, rates[field])
        states[8 * field : 8 * field + 8, :] = first
        states[8 * (fields + field) : 8 * (fields + field) + 8, :] = second
        fields_out[field] = second[2:6, :]

    place_row = lax.broadcasted_iota(jnp.int32, (32, 128), 0)
    place_lane = lax.broadcasted_iota(jnp.int32, (32, 128), 1)
    place = (place_lane == place_row + 32 * g).astype(F32).astype(BF16)
    for line in range(4):
        chosen = states[pl.ds(2 + line, 32, stride=8), :].astype(BF16)
        piece = dot(chosen, place, 0, 0).astype(BF16)
        pieces[16 * line : 16 * line + 16] = piece.reshape(16, 8, 128)

    def send_piece(k, carry):
        t = other(k)
        send(pieces.at[t], from_own.at[me], piece_send.at[0], own_recv.at[0], t, g)
        send(pieces.at[t], from_far.at[me], piece_send.at[1], far_recv.at[0], t, far)
        return carry

    lax.fori_loop(0, others, send_piece, 0)
    send(pieces.at[me], from_far.at[me], piece_send.at[1], far_recv.at[0], me, far)
    from_own[me] = pieces[me]

    def whole(source, target, send_sem, recv_sem):
        return pltpu.make_async_remote_copy(
            src_ref=source,
            dst_ref=target,
            send_sem=send_sem,
            recv_sem=recv_sem,
            device_id={"strip": me, "group": far},
            device_id_type=MESH,
        )

    most = pl.ds(0, others)
    own_all = whole(pieces.at[most], from_own.at[most], piece_send.at[0], own_recv.at[0])
    far_all = whole(pieces, from_far, piece_send.at[1], far_recv.at[0])
    own_all.wait_recv()
    far_all.wait_recv()
    half_pool[...] = from_own[...] + from_far[...]
    pool_copy = send(half_pool, core_pool, pool_send.at[0], pool_recv.at[0], me, mate)
    for copy in count_copies:
        copy.wait()
    count = jnp.sum(counts[...], axis=0)
    pool_copy.wait()
    pool = (half_pool[...] + core_pool[...]).reshape(8 * strips, 128).astype(F32).T

    moment, second_moment = out_moment[...], out_second[...]
    row_weight, row_moment, row_second = in_weight[me], in_moment[...], in_second[...]
    current = out_weight
    for turn in range(ADAM):
        step_count = PRIOR + turn + 1
        number = count[turn, 0:1, :]
        delta = ((predict - pool) * (1.0 / 512.0)).astype(BF16)
        terms[turn] = dot(current[...].reshape(hidden_width, 512), delta, 1, 1).reshape(
            strips, 8, 128
        )

        def send_terms(k, carry):
            t = other(k)
            send(
                terms.at[turn, t],
                term_in.at[turn, me],
                term_send.at[turn],
                term_recv.at[turn],
                t,
                g,
            )
            return carry

        lax.fori_loop(0, others, send_terms, 0)
        term_in[turn, me] = terms[turn, me]

        own_hidden = hidden_all[turn, pl.ds(g * (strips // 4), strips // 4)].reshape(
            hidden_width // 4, 128
        )
        grad = sum(dot(part, delta, 1, 0) for part in three_parts(own_hidden.astype(F32) * number))
        new_rows, moment, second_moment = adam_update(
            current[g], moment, second_moment, grad, step_count
        )
        following = weight_mid if turn + 1 < ADAM else out_weight_new
        following[g] = new_rows
        weight_copies = [
            send(
                following.at[g],
                following.at[g],
                weight_send.at[turn, i],
                weight_recv.at[turn, i],
                me,
                group,
            )
            for i, group in enumerate((far, mate))
        ]

        term_all = whole(
            terms.at[turn, most], term_in.at[turn, most], term_send.at[turn], term_recv.at[turn]
        )
        term_all.wait_recv()
        hidden_grad = jnp.sum(term_in[turn], axis=0)
        pre_grad = (hidden_grad * gelu_slope(own_pre)).astype(BF16)
        in_grad = sum(dot(part, code, 1, 0) for part in three_parts(pre_grad.astype(F32) * number))
        row_weight, row_moment, row_second = adam_update(
            row_weight, row_moment, row_second, in_grad, step_count
        )
        if turn + 1 < ADAM:
            own_pre = dot(row_weight, code, 1, 1)
            hidden_own[...] = gelu_value(own_pre).astype(BF16)
            source, gathered, send_sem, recv_sem = hidden_own, hidden_all.at[1], hidden_send, hidden_recv
            hidden_all[1, me] = hidden_own[...]
        else:
            rows_own[...] = row_weight
            source, gathered, send_sem, recv_sem = rows_own, in_weight_new, row_send, row_recv
            in_weight_new[me] = row_weight

        def send_rows(k, carry):
            t = other(k)
            send(source, gathered.at[me], send_sem.at[0], recv_sem.at[0], t, g)
            return carry

        lax.fori_loop(0, others, send_rows, 0)
        if turn + 1 == ADAM:
            in_moment_new[...] = row_moment
            in_second_new[...] = row_second
            out_moment_new[...] = moment
            out_second_new[...] = second_moment
        for copy in weight_copies:
            copy.wait()
        send(
            following.at[far],
            following.at[far],
            weight_send.at[turn, 2],
            weight_recv.at[turn, 2],
            me,
            mate,
        ).wait()
        rows_all = whole(gathered.at[most], gathered.at[most], send_sem.at[0], recv_sem.at[0])
        rows_all.wait()
        term_all.wait_send()
        if turn + 1 < ADAM:
            current = following
            predict = dot(
                hidden_all[1].reshape(hidden_width, 128),
                current[...].reshape(hidden_width, 512),
                0,
                0,
            )
    own_all.wait_send()
    far_all.wait_send()


def shards(
    initial,
    react_rates,
    snap_times,
    field_code,
    time_code,
    batch_ids,
    in_weight,
    in_moment,
    in_second,
    out_weight,
    out_moment,
    out_second,
):
    strips = lax.axis_size("strip")
    fields_dev = initial.shape[0]
    hidden_width = in_weight.shape[0]
    points = out_weight.shape[1]
    vmem = pl.BlockSpec(memory_space=pltpu.VMEM)
    smem = pl.BlockSpec(memory_space=pltpu.SMEM)
    dma = pltpu.SemaphoreType.DMA
    outs = pl.pallas_call(
        kernel,
        out_shape=(
            jax.ShapeDtypeStruct(initial.shape, F32),
            jax.ShapeDtypeStruct((strips, 8, in_weight.shape[1]), BF16),
            jax.ShapeDtypeStruct(in_moment.shape, F32),
            jax.ShapeDtypeStruct(in_second.shape, F32),
            jax.ShapeDtypeStruct((4, hidden_width // 4, points), BF16),
            jax.ShapeDtypeStruct(out_moment.shape, F32),
            jax.ShapeDtypeStruct(out_second.shape, F32),
        ),
        in_specs=[vmem, smem] + [vmem] * 10,
        out_specs=(vmem,) * 7,
        scratch_shapes=[
            pltpu.VMEM((2, fields_dev, 2, 128), F32),
            pltpu.VMEM((2, fields_dev, 2, 128), F32),
            pltpu.VMEM((2 * fields_dev * 8, 128), F32),
            pltpu.VMEM((strips, 8, 128), BF16),
            pltpu.VMEM((strips, 8, 128), BF16),
            pltpu.VMEM((strips, 8, 128), BF16),
            pltpu.VMEM((strips, 8, 128), BF16),
            pltpu.VMEM((strips, 8, 128), BF16),
            pltpu.VMEM((4, ADAM, 8, 128), F32),
            pltpu.VMEM((ADAM, strips, 8, 128), F32),
            pltpu.VMEM((ADAM, strips, 8, 128), F32),
            pltpu.VMEM((8, 128), BF16),
            pltpu.VMEM((ADAM, strips, 8, 128), BF16),
            pltpu.VMEM((8, in_weight.shape[1]), BF16),
            pltpu.VMEM((4, hidden_width // 4, points), BF16),
            dma((2,)),
            dma((2,)),
            dma((2,)),
            dma((1,)),
            dma((1,)),
            dma((1,)),
            dma((1,)),
            dma((3,)),
            dma((3,)),
            dma((ADAM,)),
            dma((ADAM,)),
            dma((1,)),
            dma((1,)),
            dma((ADAM, 3)),
            dma((ADAM, 3)),
            dma((1,)),
            dma((1,)),
        ],
        compiler_params=pltpu.CompilerParams(
            collective_id=0, has_side_effects=True, vmem_limit_bytes=48 * 1024 * 1024
        ),
        name="ensemble",
    )(
        initial,
        react_rates,
        jnp.transpose(snap_times),
        field_code,
        time_code,
        batch_ids,
        in_weight.reshape(strips, hidden_width // strips, in_weight.shape[1]),
        in_moment,
        in_second,
        out_weight.reshape(4, hidden_width // 4, points),
        out_moment,
        out_second,
    )
    fields, in_new, in_m, in_v, out_new, out_m, out_v = outs
    return (
        fields,
        in_new.reshape(in_weight.shape),
        in_m,
        in_v,
        out_new.reshape(out_weight.shape),
        out_m,
        out_v,
    )


def solution(mesh):
    in_specs = (
        P("group", "strip", None),
        P("group"),
        P(),
        P(),
        P(),
        P(None, "group"),
        P(),
        P("strip", None),
        P("strip", None),
        P(None, "strip"),
        P("group", "strip"),
        P("group", "strip"),
    )
    out_specs = (
        P("group", "strip", None),
        P(),
        P("strip", None),
        P("strip", None),
        P(None, "strip"),
        P("group", "strip"),
        P("group", "strip"),
    )
    return jax.shard_map(shards, mesh=mesh, in_specs=in_specs, out_specs=out_specs, check_vma=False)
```

```python
import functools

import jax
import jax.numpy as jnp
from jax import lax
from jax.experimental import pallas as pl
from jax.experimental.pallas import tpu as pltpu
from jax.sharding import PartitionSpec as P

STEPS = 2
SNAPS = 4
ADAM = 2
PRIOR = 100

DIFF_ROWS = 0.35
DIFF_COLS = 0.05
BETA_ONE = 0.9
BETA_TWO = 0.999
LEARN_RATE = 0.003
EPSILON = 1e-08
GELU_SCALE = 0.7978845608
GELU_CUBE = 0.044715

MESH = pl.DeviceIdType.MESH
F32 = jnp.float32
BF16 = jnp.bfloat16


def gelu_value(pre_act):
    return (
        0.5
        * pre_act
        * (1.0 + jnp.tanh(GELU_SCALE * (pre_act + GELU_CUBE * pre_act * pre_act * pre_act)))
    )


def gelu_slope(pre_act):
    tanh_part = jnp.tanh(GELU_SCALE * (pre_act + GELU_CUBE * pre_act * pre_act * pre_act))
    return 0.5 * (1.0 + tanh_part) + 0.5 * pre_act * (1.0 - tanh_part * tanh_part) * GELU_SCALE * (
        1.0 + 3.0 * GELU_CUBE * pre_act * pre_act
    )


def adam_update(weight, moment, second, gradient, step_count):
    moment = BETA_ONE * moment + (1.0 - BETA_ONE) * gradient
    second = BETA_TWO * second + (1.0 - BETA_TWO) * gradient * gradient
    update = (
        moment
        / (1.0 - BETA_ONE**step_count)
        / (jnp.sqrt(second / (1.0 - BETA_TWO**step_count)) + EPSILON)
    )
    return ((weight.astype(F32) - LEARN_RATE * update).astype(BF16), moment, second)


def dot(left, right, left_dim, right_dim):
    return lax.dot_general(
        left, right, (((left_dim,), (right_dim,)), ((), ())), preferred_element_type=F32
    )


def three_parts(value):
    high = value.astype(BF16)
    rest = value - high.astype(F32)
    middle = rest.astype(BF16)
    low = (rest - middle.astype(F32)).astype(BF16)
    return high, middle, low


def kernel(
    initial_hbm,
    rates_hbm,
    times_hbm,
    field_code_hbm,
    time_code_hbm,
    batch_ids_hbm,
    in_weight_hbm,
    in_moment_hbm,
    in_second_hbm,
    out_weight_hbm,
    out_moment_hbm,
    out_second_hbm,
    fields_out,
    in_weight_new,
    in_moment_new,
    in_second_new,
    out_weight_new,
    out_moment_new,
    out_second_new,
    initial,
    rates,
    times,
    field_code,
    time_code,
    batch_ids,
    in_weight,
    in_moment,
    in_second,
    out_weight,
    out_moment,
    out_second,
    edges,
    halo,
    states,
    pieces,
    from_own,
    from_far,
    half_pool,
    core_pool,
    counts,
    terms,
    term_in,
    hidden_own,
    hidden_all,
    rows_own,
    weight_mid,
    halo_send,
    halo_recv,
    piece_send,
    own_recv,
    far_recv,
    pool_send,
    pool_recv,
    count_send,
    count_recv,
    term_send,
    term_recv,
    hidden_send,
    hidden_recv,
    weight_send,
    weight_recv,
    row_send,
    row_recv,
    load_sem,
):
    strips = lax.axis_size("strip")
    me = lax.axis_index("strip")
    g = lax.axis_index("group")
    far = lax.rem(g + 2, 4)
    mate = g + 1 - 2 * lax.rem(g, 2)
    far_mate = lax.rem(mate + 2, 4)
    fields = initial.shape[0]
    others = strips - 1

    def other(k):
        return lax.rem(me + 1 + k, strips)

    def send(source, target, send_sem, recv_sem, strip, group):
        copy = pltpu.make_async_remote_copy(
            src_ref=source,
            dst_ref=target,
            send_sem=send_sem,
            recv_sem=recv_sem,
            device_id={"strip": strip, "group": group},
            device_id_type=MESH,
        )
        copy.start()
        return copy

    loads = [
        pltpu.make_async_copy(source, target, load_sem.at[i])
        for i, (source, target) in enumerate(
            (
                (initial_hbm, initial),
                (batch_ids_hbm, batch_ids),
                (times_hbm, times),
                (field_code_hbm, field_code),
                (time_code_hbm, time_code),
                (in_weight_hbm, in_weight),
                (rates_hbm, rates),
                (out_weight_hbm, out_weight),
                (in_moment_hbm, in_moment),
                (in_second_hbm, in_second),
                (out_moment_hbm, out_moment),
                (out_second_hbm, out_second),
            )
        )
    ]
    for load in loads:
        load.start()

    barrier = pltpu.get_barrier_semaphore()

    def greet(strip, group):
        pl.semaphore_signal(
            barrier, inc=1, device_id={"strip": strip, "group": group}, device_id_type=MESH
        )

    def greet_strip(k, carry):
        greet(other(k), g)
        greet(other(k), far)
        return carry

    lax.fori_loop(0, others, greet_strip, 0)
    greet(me, far)
    greet(me, mate)
    greet(me, far_mate)

    for load in loads[:3]:
        load.wait()
    edges[0] = initial[:, 0:2, :]
    edges[1] = initial[:, 2:4, :]

    kind_row = lax.broadcasted_iota(jnp.int32, (128, 128), 0)
    field_row = 16 * (kind_row // 32) + lax.rem(kind_row, 16)
    kind_lane = lax.broadcasted_iota(jnp.int32, (64, 128), 1)
    field_lane = 16 * (kind_lane // 32) + lax.rem(kind_lane, 16)
    spread = (lax.broadcasted_iota(jnp.int32, (64, 128), 0) == field_lane).astype(F32).astype(BF16)
    kind_times = dot(times[...].astype(F32).astype(BF16), spread, 1, 0)
    slot = lax.broadcasted_iota(jnp.int32, (4, 128), 0)
    own_time = jnp.sum(jnp.where(slot == g, kind_times, 0.0), axis=0, keepdims=True)
    step_lane = (lax.rem(lax.broadcasted_iota(jnp.int32, (1, 128), 1) // 16, 2) + 1).astype(F32)
    time_fits = jnp.where(own_time == step_lane, 1.0, 0.0)
    ones = jnp.ones((8, 128), BF16)
    for turn in range(ADAM):
        hits = (batch_ids[turn : turn + 1, :] == field_row).astype(F32).astype(BF16)
        counts[0, turn] = dot(ones, hits, 1, 1) * time_fits

    for load in loads[3:6]:
        load.wait()
    code_parts = []
    for part in range(4):
        for step in range(STEPS):
            code_parts.append(
                (
                    field_code[16 * part : 16 * part + 16, :].astype(F32)
                    + time_code[step : step + 1, :].astype(F32)
                ).astype(BF16)
            )
    code = jnp.concatenate(code_parts, axis=0)
    hidden_width = 8 * strips
    pre_act = dot(in_weight[...].reshape(hidden_width, 512), code, 1, 1)
    hidden = gelu_value(pre_act).astype(BF16)
    hidden_all[0] = hidden.reshape(strips, 8, 128)

    pl.semaphore_wait(barrier, 2 * others + 3)

    up = lax.rem(me + others, strips)
    down = lax.rem(me + 1, strips)
    halo_copies = [
        send(edges.at[0], halo.at[1], halo_send.at[0], halo_recv.at[1], up, g),
        send(edges.at[1], halo.at[0], halo_send.at[1], halo_recv.at[0], down, g),
    ]
    count_copies = [
        send(counts.at[0], counts.at[1 + i], count_send.at[i], count_recv.at[i], me, group)
        for i, group in enumerate((far, mate, far_mate))
    ]

    for load in loads[6:]:
        load.wait()
    old_weight = out_weight[...].reshape(hidden_width, 512)
    predict = dot(hidden, old_weight, 0, 0)
    own_pre = dot(in_weight[me], code, 1, 1)

    for copy in halo_copies:
        copy.wait()

    row = lax.broadcasted_iota(jnp.int32, (8, 128), 0) + 4 * me - 2
    inside = jnp.logical_and(row >= 0, row < 4 * strips)

    def advance(center, rate):
        across = pltpu.roll(center, 1, 1) + pltpu.roll(center, 127, 1)
        return (
            center
            + DIFF_ROWS * (pltpu.roll(center, 1, 0) + pltpu.roll(center, 7, 0) - 2.0 * center)
            + DIFF_COLS * (across - 2.0 * center)
            + rate * center * (1.0 - center * center)
        )

    for field in range(fields):
        start = jnp.concatenate([halo[0, field], initial[field], halo[1, field]], axis=0)
        start = jnp.where(inside, start, 0.0)
        first = jnp.where(inside, advance(start, rates[field]), 0.0)
        second = advance(first, rates[field])
        states[8 * field : 8 * field + 8, :] = first
        states[8 * (fields + field) : 8 * (fields + field) + 8, :] = second
        fields_out[field] = second[2:6, :]

    place_row = lax.broadcasted_iota(jnp.int32, (32, 128), 0)
    place_lane = lax.broadcasted_iota(jnp.int32, (32, 128), 1)
    place = (place_lane == place_row + 32 * g).astype(F32).astype(BF16)
    for line in range(4):
        chosen = states[pl.ds(2 + line, 32, stride=8), :].astype(BF16)
        piece = dot(chosen, place, 0, 0).astype(BF16)
        pieces[16 * line : 16 * line + 16] = piece.reshape(16, 8, 128)

    def send_piece(k, carry):
        t = other(k)
        send(pieces.at[t], from_own.at[me], piece_send.at[0], own_recv.at[0], t, g)
        send(pieces.at[t], from_far.at[me], piece_send.at[1], far_recv.at[0], t, far)
        return carry

    lax.fori_loop(0, others, send_piece, 0)
    send(pieces.at[me], from_far.at[me], piece_send.at[1], far_recv.at[0], me, far)
    from_own[me] = pieces[me]

    def whole(source, target, send_sem, recv_sem):
        return pltpu.make_async_remote_copy(
            src_ref=source,
            dst_ref=target,
            send_sem=send_sem,
            recv_sem=recv_sem,
            device_id={"strip": me, "group": far},
            device_id_type=MESH,
        )

    most = pl.ds(0, others)
    own_all = whole(pieces.at[most], from_own.at[most], piece_send.at[0], own_recv.at[0])
    far_all = whole(pieces, from_far, piece_send.at[1], far_recv.at[0])
    own_all.wait_recv()
    far_all.wait_recv()
    half_pool[...] = from_own[...] + from_far[...]
    pool_copy = send(half_pool, core_pool, pool_send.at[0], pool_recv.at[0], me, mate)
    for copy in count_copies:
        copy.wait()
    count = jnp.sum(counts[...], axis=0)
    pool_copy.wait()
    pool = (half_pool[...] + core_pool[...]).reshape(8 * strips, 128).astype(F32).T

    moment, second_moment = out_moment[...], out_second[...]
    row_weight, row_moment, row_second = in_weight[me], in_moment[...], in_second[...]
    current = out_weight
    for turn in range(ADAM):
        step_count = PRIOR + turn + 1
        number = count[turn, 0:1, :]
        delta = ((predict - pool) * (1.0 / 512.0)).astype(BF16)
        terms[turn] = dot(current[...].reshape(hidden_width, 512), delta, 1, 1).reshape(
            strips, 8, 128
        )

        def send_terms(k, carry):
            t = other(k)
            send(
                terms.at[turn, t],
                term_in.at[turn, me],
                term_send.at[turn],
                term_recv.at[turn],
                t,
                g,
            )
            return carry

        lax.fori_loop(0, others, send_terms, 0)
        term_in[turn, me] = terms[turn, me]

        own_hidden = hidden_all[turn, pl.ds(g * (strips // 4), strips // 4)].reshape(
            hidden_width // 4, 128
        )
        grad = sum(dot(part, delta, 1, 0) for part in three_parts(own_hidden.astype(F32) * number))
        new_rows, moment, second_moment = adam_update(
            current[g], moment, second_moment, grad, step_count
        )
        following = weight_mid if turn + 1 < ADAM else out_weight_new
        following[g] = new_rows
        weight_copies = [
            send(
                following.at[g],
                following.at[g],
                weight_send.at[turn, i],
                weight_recv.at[turn, i],
                me,
                group,
            )
            for i, group in enumerate((far, mate))
        ]

        term_all = whole(
            terms.at[turn, most], term_in.at[turn, most], term_send.at[turn], term_recv.at[turn]
        )
        term_all.wait_recv()
        hidden_grad = jnp.sum(term_in[turn], axis=0)
        pre_grad = (hidden_grad * gelu_slope(own_pre)).astype(BF16)
        in_grad = sum(dot(part, code, 1, 0) for part in three_parts(pre_grad.astype(F32) * number))
        row_weight, row_moment, row_second = adam_update(
            row_weight, row_moment, row_second, in_grad, step_count
        )
        if turn + 1 < ADAM:
            own_pre = dot(row_weight, code, 1, 1)
            hidden_own[...] = gelu_value(own_pre).astype(BF16)
            source, gathered, send_sem, recv_sem = hidden_own, hidden_all.at[1], hidden_send, hidden_recv
            hidden_all[1, me] = hidden_own[...]
        else:
            rows_own[...] = row_weight
            source, gathered, send_sem, recv_sem = rows_own, in_weight_new, row_send, row_recv
            in_weight_new[me] = row_weight

        def send_rows(k, carry):
            t = other(k)
            send(source, gathered.at[me], send_sem.at[0], recv_sem.at[0], t, g)
            return carry

        lax.fori_loop(0, others, send_rows, 0)
        if turn + 1 == ADAM:
            in_moment_new[...] = row_moment
            in_second_new[...] = row_second
            out_moment_new[...] = moment
            out_second_new[...] = second_moment
        for copy in weight_copies:
            copy.wait()
        send(
            following.at[far],
            following.at[far],
            weight_send.at[turn, 2],
            weight_recv.at[turn, 2],
            me,
            mate,
        ).wait()
        rows_all = whole(gathered.at[most], gathered.at[most], send_sem.at[0], recv_sem.at[0])
        rows_all.wait()
        term_all.wait_send()
        if turn + 1 < ADAM:
            current = following
            predict = dot(
                hidden_all[1].reshape(hidden_width, 128),
                current[...].reshape(hidden_width, 512),
                0,
                0,
            )
    own_all.wait_send()
    far_all.wait_send()


def keep(sources, targets, sem):
    copies = [
        pltpu.make_async_copy(source, target, sem.at[i])
        for i, (source, target) in enumerate(zip(sources, targets))
    ]
    for copy in copies:
        copy.start()
    for copy in copies:
        copy.wait()


def store(*refs):
    count = len(refs) // 2
    keep(refs[:count], refs[count : 2 * count], refs[-1])


def shards(
    initial,
    react_rates,
    snap_times,
    field_code,
    time_code,
    batch_ids,
    in_weight,
    in_moment,
    in_second,
    out_weight,
    out_moment,
    out_second,
):
    strips = lax.axis_size("strip")
    fields_dev = initial.shape[0]
    hidden_width = in_weight.shape[0]
    points = out_weight.shape[1]
    vmem = pl.BlockSpec(memory_space=pltpu.VMEM)
    hbm = pl.BlockSpec(memory_space=pltpu.HBM)
    dma = pltpu.SemaphoreType.DMA
    outs = pl.pallas_call(
        kernel,
        out_shape=(
            pltpu.VMEM(initial.shape, F32),
            pltpu.VMEM((strips, 8, in_weight.shape[1]), BF16),
            pltpu.VMEM(in_moment.shape, F32),
            pltpu.VMEM(in_second.shape, F32),
            pltpu.VMEM((4, hidden_width // 4, points), BF16),
            pltpu.VMEM(out_moment.shape, F32),
            pltpu.VMEM(out_second.shape, F32),
        ),
        in_specs=[hbm] * 12,
        out_specs=(vmem,) * 7,
        scratch_shapes=[
            pltpu.VMEM(initial.shape, F32),
            pltpu.SMEM(react_rates.shape, F32),
            pltpu.VMEM(snap_times.shape[::-1], jnp.int32),
            pltpu.VMEM(field_code.shape, BF16),
            pltpu.VMEM(time_code.shape, BF16),
            pltpu.VMEM(batch_ids.shape, jnp.int32),
            pltpu.VMEM((strips, 8, in_weight.shape[1]), BF16),
            pltpu.VMEM(in_moment.shape, F32),
            pltpu.VMEM(in_second.shape, F32),
            pltpu.VMEM((4, hidden_width // 4, points), BF16),
            pltpu.VMEM(out_moment.shape, F32),
            pltpu.VMEM(out_second.shape, F32),
            pltpu.VMEM((2, fields_dev, 2, 128), F32),
            pltpu.VMEM((2, fields_dev, 2, 128), F32),
            pltpu.VMEM((2 * fields_dev * 8, 128), F32),
            pltpu.VMEM((strips, 8, 128), BF16),
            pltpu.VMEM((strips, 8, 128), BF16),
            pltpu.VMEM((strips, 8, 128), BF16),
            pltpu.VMEM((strips, 8, 128), BF16),
            pltpu.VMEM((strips, 8, 128), BF16),
            pltpu.VMEM((4, ADAM, 8, 128), F32),
            pltpu.VMEM((ADAM, strips, 8, 128), F32),
            pltpu.VMEM((ADAM, strips, 8, 128), F32),
            pltpu.VMEM((8, 128), BF16),
            pltpu.VMEM((ADAM, strips, 8, 128), BF16),
            pltpu.VMEM((8, in_weight.shape[1]), BF16),
            pltpu.VMEM((4, hidden_width // 4, points), BF16),
            dma((2,)),
            dma((2,)),
            dma((2,)),
            dma((1,)),
            dma((1,)),
            dma((1,)),
            dma((1,)),
            dma((3,)),
            dma((3,)),
            dma((ADAM,)),
            dma((ADAM,)),
            dma((1,)),
            dma((1,)),
            dma((ADAM, 3)),
            dma((ADAM, 3)),
            dma((1,)),
            dma((1,)),
            dma((12,)),
        ],
        compiler_params=pltpu.CompilerParams(
            collective_id=0, has_side_effects=True, vmem_limit_bytes=48 * 1024 * 1024
        ),
        name="ensemble",
    )(
        *(
            pltpu.with_memory_space_constraint(operand, pltpu.HBM)
            for operand in (
        initial,
        react_rates,
        jnp.transpose(snap_times),
        field_code,
        time_code,
        batch_ids,
        in_weight.reshape(strips, hidden_width // strips, in_weight.shape[1]),
        in_moment,
        in_second,
        out_weight.reshape(4, hidden_width // 4, points),
        out_moment,
        out_second,
            )
        )
    )
    outs = pl.pallas_call(
        store,
        out_shape=tuple(pltpu.HBM(out.shape, out.dtype) for out in outs),
        in_specs=[vmem] * 7,
        out_specs=(hbm,) * 7,
        scratch_shapes=[dma((7,))],
        name="store",
    )(*(pltpu.with_memory_space_constraint(out, pltpu.VMEM) for out in outs))
    fields, in_new, in_m, in_v, out_new, out_m, out_v = outs
    return (
        fields,
        in_new.reshape(in_weight.shape),
        in_m,
        in_v,
        out_new.reshape(out_weight.shape),
        out_m,
        out_v,
    )


def solution(mesh):
    in_specs = (
        P("group", "strip", None),
        P("group"),
        P(),
        P(),
        P(),
        P(None, "group"),
        P(),
        P("strip", None),
        P("strip", None),
        P(None, "strip"),
        P("group", "strip"),
        P("group", "strip"),
    )
    out_specs = (
        P("group", "strip", None),
        P(),
        P("strip", None),
        P("strip", None),
        P(None, "strip"),
        P("group", "strip"),
        P("group", "strip"),
    )
    return jax.shard_map(shards, mesh=mesh, in_specs=in_specs, out_specs=out_specs, check_vma=False)
```

```python
import functools

import jax
import jax.numpy as jnp
from jax import lax
from jax.experimental import pallas as pl
from jax.experimental.pallas import tpu as pltpu
from jax.sharding import PartitionSpec as P

STEPS = 2
SNAPS = 4
ADAM = 2
PRIOR = 100

DIFF_ROWS = 0.35
DIFF_COLS = 0.05
BETA_ONE = 0.9
BETA_TWO = 0.999
LEARN_RATE = 0.003
EPSILON = 1e-08
GELU_SCALE = 0.7978845608
GELU_CUBE = 0.044715

MESH = pl.DeviceIdType.MESH
F32 = jnp.float32
BF16 = jnp.bfloat16


def gelu_value(pre_act):
    return (
        0.5
        * pre_act
        * (1.0 + jnp.tanh(GELU_SCALE * (pre_act + GELU_CUBE * pre_act * pre_act * pre_act)))
    )


def gelu_slope(pre_act):
    tanh_part = jnp.tanh(GELU_SCALE * (pre_act + GELU_CUBE * pre_act * pre_act * pre_act))
    return 0.5 * (1.0 + tanh_part) + 0.5 * pre_act * (1.0 - tanh_part * tanh_part) * GELU_SCALE * (
        1.0 + 3.0 * GELU_CUBE * pre_act * pre_act
    )


def adam_update(weight, moment, second, gradient, step_count):
    moment = BETA_ONE * moment + (1.0 - BETA_ONE) * gradient
    second = BETA_TWO * second + (1.0 - BETA_TWO) * gradient * gradient
    update = (
        moment
        / (1.0 - BETA_ONE**step_count)
        / (jnp.sqrt(second / (1.0 - BETA_TWO**step_count)) + EPSILON)
    )
    return ((weight.astype(F32) - LEARN_RATE * update).astype(BF16), moment, second)


def dot(left, right, left_dim, right_dim):
    return lax.dot_general(
        left, right, (((left_dim,), (right_dim,)), ((), ())), preferred_element_type=F32
    )


def three_parts(value):
    high = value.astype(BF16)
    rest = value - high.astype(F32)
    middle = rest.astype(BF16)
    low = (rest - middle.astype(F32)).astype(BF16)
    return high, middle, low


def kernel(
    initial_hbm,
    rates_hbm,
    times_hbm,
    field_code_hbm,
    time_code_hbm,
    batch_ids_hbm,
    in_weight_hbm,
    in_moment_hbm,
    in_second_hbm,
    out_weight_hbm,
    out_moment_hbm,
    out_second_hbm,
    fields_out,
    in_weight_new,
    in_moment_new,
    in_second_new,
    out_weight_new,
    out_moment_new,
    out_second_new,
    initial,
    rates,
    times,
    field_code,
    time_code,
    batch_ids,
    in_weight,
    in_moment,
    in_second,
    out_weight,
    out_moment,
    out_second,
    edges,
    halo,
    states,
    pieces,
    arrived,
    counts,
    terms,
    plane_in,
    line_out,
    line_in,
    hidden_own,
    hidden_all,
    weight_mid,
    halo_send,
    halo_recv,
    piece_send,
    own_recv,
    far_recv,
    pool_send,
    pool_recv,
    count_send,
    count_recv,
    plane_send,
    plane_recv,
    line_send,
    line_recv,
    hidden_send,
    hidden_recv,
    weight_send,
    weight_recv,
    row_send,
    row_recv,
    load_sem,
):
    strips = lax.axis_size("strip")
    me = lax.axis_index("strip")
    g = lax.axis_index("group")
    far = lax.rem(g + 2, 4)
    mate = g + 1 - 2 * lax.rem(g, 2)
    far_mate = lax.rem(mate + 2, 4)
    fields = initial.shape[0]
    others = strips - 1
    at_y, at_z, at_x = me // 16, lax.rem(me // 4, 4), lax.rem(me, 4)

    def other(k):
        return lax.rem(me + 1 + k, strips)

    def send(source, target, send_sem, recv_sem, strip, group):
        copy = pltpu.make_async_remote_copy(
            src_ref=source,
            dst_ref=target,
            send_sem=send_sem,
            recv_sem=recv_sem,
            device_id={"strip": strip, "group": group},
            device_id_type=MESH,
        )
        copy.start()
        return copy

    loads = [
        pltpu.make_async_copy(source, target, load_sem.at[i])
        for i, (source, target) in enumerate(
            (
                (initial_hbm, initial),
                (batch_ids_hbm, batch_ids),
                (times_hbm, times),
                (field_code_hbm, field_code),
                (time_code_hbm, time_code),
                (in_weight_hbm, in_weight),
                (rates_hbm, rates),
                (out_weight_hbm, out_weight),
                (in_moment_hbm, in_moment),
                (in_second_hbm, in_second),
                (out_moment_hbm, out_moment),
                (out_second_hbm, out_second),
            )
        )
    ]
    for load in loads:
        load.start()

    barrier = pltpu.get_barrier_semaphore()

    def greet(strip, group):
        pl.semaphore_signal(
            barrier, inc=1, device_id={"strip": strip, "group": group}, device_id_type=MESH
        )

    def greet_strip(k, carry):
        greet(other(k), g)
        greet(other(k), far)
        return carry

    lax.fori_loop(0, others, greet_strip, 0)
    greet(me, far)
    greet(me, mate)
    greet(me, far_mate)

    for load in loads[:3]:
        load.wait()
    edges[0] = initial[:, 0:2, :]
    edges[1] = initial[:, 2:4, :]

    kind_row = lax.broadcasted_iota(jnp.int32, (128, 128), 0)
    field_row = 16 * (kind_row // 32) + lax.rem(kind_row, 16)
    kind_lane = lax.broadcasted_iota(jnp.int32, (64, 128), 1)
    field_lane = 16 * (kind_lane // 32) + lax.rem(kind_lane, 16)
    spread = (lax.broadcasted_iota(jnp.int32, (64, 128), 0) == field_lane).astype(F32).astype(BF16)
    kind_times = dot(times[...].astype(F32).astype(BF16), spread, 1, 0)
    slot = lax.broadcasted_iota(jnp.int32, (4, 128), 0)
    own_time = jnp.sum(jnp.where(slot == g, kind_times, 0.0), axis=0, keepdims=True)
    step_lane = (lax.rem(lax.broadcasted_iota(jnp.int32, (1, 128), 1) // 16, 2) + 1).astype(F32)
    time_fits = jnp.where(own_time == step_lane, 1.0, 0.0)
    ones = jnp.ones((8, 128), BF16)
    for turn in range(ADAM):
        hits = (batch_ids[turn : turn + 1, :] == field_row).astype(F32).astype(BF16)
        counts[0, turn] = dot(ones, hits, 1, 1) * time_fits

    for load in loads[3:6]:
        load.wait()
    code_parts = []
    for part in range(4):
        for step in range(STEPS):
            code_parts.append(
                (
                    field_code[16 * part : 16 * part + 16, :].astype(F32)
                    + time_code[step : step + 1, :].astype(F32)
                ).astype(BF16)
            )
    code = jnp.concatenate(code_parts, axis=0)
    hidden_width = 8 * strips
    pre_act = dot(in_weight[...].reshape(hidden_width, 512), code, 1, 1)
    hidden = gelu_value(pre_act).astype(BF16)
    hidden_all[0] = hidden.reshape(strips, 8, 128)

    pl.semaphore_wait(barrier, 2 * others + 3)

    up = lax.rem(me + others, strips)
    down = lax.rem(me + 1, strips)
    halo_copies = [
        send(edges.at[0], halo.at[1], halo_send.at[0], halo_recv.at[1], up, g),
        send(edges.at[1], halo.at[0], halo_send.at[1], halo_recv.at[0], down, g),
    ]
    count_copies = [
        send(counts.at[0], counts.at[1 + i], count_send.at[i], count_recv.at[i], me, group)
        for i, group in enumerate((far, mate, far_mate))
    ]

    for load in loads[6:]:
        load.wait()
    old_weight = out_weight[...].reshape(hidden_width, 512)
    predict = dot(hidden, old_weight, 0, 0)
    own_pre = dot(in_weight[me], code, 1, 1)

    for copy in halo_copies:
        copy.wait()

    row = lax.broadcasted_iota(jnp.int32, (8, 128), 0) + 4 * me - 2
    inside = jnp.logical_and(row >= 0, row < 4 * strips)

    def advance(center, rate):
        across = pltpu.roll(center, 1, 1) + pltpu.roll(center, 127, 1)
        return (
            center
            + DIFF_ROWS * (pltpu.roll(center, 1, 0) + pltpu.roll(center, 7, 0) - 2.0 * center)
            + DIFF_COLS * (across - 2.0 * center)
            + rate * center * (1.0 - center * center)
        )

    for field in range(fields):
        start = jnp.concatenate([halo[0, field], initial[field], halo[1, field]], axis=0)
        start = jnp.where(inside, start, 0.0)
        first = jnp.where(inside, advance(start, rates[field]), 0.0)
        second = advance(first, rates[field])
        states[8 * field : 8 * field + 8, :] = first
        states[8 * (fields + field) : 8 * (fields + field) + 8, :] = second
        fields_out[field] = second[2:6, :]

    def grid(shape):
        return (lax.broadcasted_iota(jnp.int32, shape, i) for i in range(2))

    def one_hot(hit):
        return jnp.where(hit, 1.0, 0.0).astype(BF16)

    kind_at, lane_at = grid((32, 128))
    repeat = one_hot(kind_at == lax.rem(lane_at, 32))
    point_at, lane_at = grid((128, 128))
    own_lanes = lax.rem(point_at, 4) == lane_at // 32
    four_at, point_at = grid((32, 128))
    fold = one_hot(four_at == point_at // 4)
    for line in range(4):
        chosen = states[pl.ds(2 + line, 32, stride=8), :].astype(BF16)
        spread_out = jnp.where(own_lanes, dot(chosen, repeat, 0, 0), 0.0).astype(BF16)
        piece = dot(fold, spread_out, 1, 0)
        pieces[16 * line : 16 * line + 16] = piece.reshape(16, 2, 128).astype(BF16)

    def send_piece(k, carry):
        t = other(k)
        send(pieces.at[t], arrived.at[0, me], piece_send.at[0], own_recv.at[0], t, g)
        send(pieces.at[t], arrived.at[1, me], piece_send.at[1], far_recv.at[0], t, far)
        return carry

    lax.fori_loop(0, others, send_piece, 0)
    send(pieces.at[me], arrived.at[1, me], piece_send.at[1], far_recv.at[0], me, far)
    arrived[0, me] = pieces[me]

    def whole(source, target, send_sem, recv_sem):
        return pltpu.make_async_remote_copy(
            src_ref=source,
            dst_ref=target,
            send_sem=send_sem,
            recv_sem=recv_sem,
            device_id={"strip": me, "group": far},
            device_id_type=MESH,
        )

    most = pl.ds(0, others)
    own_all = whole(pieces.at[most], arrived.at[0, most], piece_send.at[0], own_recv.at[0])
    far_all = whole(pieces, arrived.at[1], piece_send.at[1], far_recv.at[0])
    own_all.wait_recv()
    far_all.wait_recv()
    pool_copy = send(
        arrived.at[pl.ds(0, 2)], arrived.at[pl.ds(2, 2)], pool_send.at[0], pool_recv.at[0], me, mate
    )
    for copy in count_copies:
        copy.wait()
    count = jnp.sum(counts[...], axis=0)
    point_at, row_at = grid((8 * strips, 2 * strips))
    unfold = one_hot(point_at // 4 == row_at)
    point_at, lane_at = grid((8 * strips, 128))
    own_lanes = lax.rem(point_at, 4) == lane_at // 32
    lane_at, kind_at = grid((128, 128))

    def pool_of(part, group):
        rows = arrived[part].astype(F32).reshape(2 * strips, 128).astype(BF16)
        points = jnp.where(own_lanes, dot(unfold, rows, 1, 0), 0.0).astype(BF16)
        return dot(one_hot(kind_at == 32 * group + lax.rem(lane_at, 32)), points, 0, 1)

    pool = pool_of(0, g) + pool_of(1, far)
    pool_copy.wait()
    pool = pool + pool_of(2, mate) + pool_of(3, far_mate)

    moment, second_moment = out_moment[...], out_second[...]
    row_weight, row_moment, row_second = in_weight[me], in_moment[...], in_second[...]
    current = out_weight
    for turn in range(ADAM):
        step_count = PRIOR + turn + 1
        number = count[turn, 0:1, :]
        delta = ((predict - pool) * (1.0 / 512.0)).astype(BF16)
        weights = current[...].reshape(hidden_width, 512)

        own_hidden = hidden_all[turn, pl.ds(g * (strips // 4), strips // 4)].reshape(
            hidden_width // 4, 128
        )
        grad = sum(dot(part, delta, 1, 0) for part in three_parts(own_hidden.astype(F32) * number))
        new_rows, moment, second_moment = adam_update(
            current[g], moment, second_moment, grad, step_count
        )
        following = weight_mid if turn + 1 < ADAM else out_weight_new
        following[g] = new_rows

        def weight_copy(part, i, group):
            return send(
                following.at[part],
                following.at[part],
                weight_send.at[turn, i],
                weight_recv.at[turn, i],
                me,
                group,
            )

        def start_weight():
            return [weight_copy(g, 0, far), weight_copy(g, 1, mate)]

        weight_copies = start_weight()
        terms[turn] = dot(weights, delta, 1, 1).reshape(4, 4, 4, 8, 128)

        def send_terms(k, carry):
            ty = lax.rem(at_y + (k + 1) // 4, 4)
            tx = lax.rem(at_x + lax.rem(k + 1, 4), 4)
            send(
                terms.at[turn, ty, :, tx],
                plane_in.at[turn, 4 * at_y + at_x],
                plane_send.at[turn],
                plane_recv.at[turn],
                16 * ty + 4 * at_z + tx,
                g,
            )
            return carry

        lax.fori_loop(0, 15, send_terms, 0)
        plane_in[turn, 4 * at_y + at_x] = terms[turn, at_y, :, at_x]
        plane = plane_in.at[turn, pl.ds(0, 15)]
        plane_all = whole(plane, plane, plane_send.at[turn], plane_recv.at[turn])
        plane_all.wait_recv()
        line_out[turn] = jnp.sum(plane_in[turn], axis=0)

        def send_line(k, carry):
            tz = lax.rem(at_z + k + 1, 4)
            send(
                line_out.at[turn, tz],
                line_in.at[turn, at_z],
                line_send.at[turn],
                line_recv.at[turn],
                16 * at_y + 4 * tz + at_x,
                g,
            )
            return carry

        lax.fori_loop(0, 3, send_line, 0)
        line_in[turn, at_z] = line_out[turn, at_z]
        line = line_in.at[turn, pl.ds(0, 3)]
        line_all = whole(line, line, line_send.at[turn], line_recv.at[turn])
        line_all.wait_recv()

        hidden_grad = jnp.sum(line_in[turn], axis=0)
        pre_grad = (hidden_grad * gelu_slope(own_pre)).astype(BF16)
        in_grad = sum(dot(part, code, 1, 0) for part in three_parts(pre_grad.astype(F32) * number))
        row_weight, row_moment, row_second = adam_update(
            row_weight, row_moment, row_second, in_grad, step_count
        )
        if turn + 1 < ADAM:
            own_pre = dot(row_weight, code, 1, 1)
            hidden_own[...] = gelu_value(own_pre).astype(BF16)
            hidden_all[1, me] = hidden_own[...]
            source, target, several = hidden_own, hidden_all.at[1, me], hidden_all.at[1, most]
            send_sem, recv_sem = hidden_send, hidden_recv
        else:
            half = pl.ds(pl.multiple_of(256 * lax.rem(g, 2), 256), 256)
            in_weight_new[me, :, half] = jnp.where(
                lax.rem(g, 2) == 0,
                row_weight[:, :256].astype(F32),
                row_weight[:, 256:].astype(F32),
            ).astype(BF16)
            source = target = in_weight_new.at[me, :, half]
            several = in_weight_new.at[most, :, half]
            send_sem, recv_sem = row_send, row_recv


        def send_rows(k, carry):
            t = other(k)
            send(source, target, send_sem.at[0], recv_sem.at[0], t, g)
            return carry

        lax.fori_loop(0, others, send_rows, 0)
        if turn + 1 == ADAM:
            in_moment_new[...] = row_moment
            in_second_new[...] = row_second
            out_moment_new[...] = moment
            out_second_new[...] = second_moment
        weight_copies[0].wait()
        weight_copies.append(weight_copy(far, 2, mate))
        rows_all = whole(several, several, send_sem.at[0], recv_sem.at[0])
        rows_all.wait()
        if turn + 1 == ADAM:
            columns = in_weight_new.at[:, :, half]
            send(columns, columns, row_send.at[1], row_recv.at[1], me, mate).wait()
        for copy in weight_copies[1:]:
            copy.wait()
        plane_all.wait_send()
        line_all.wait_send()
        if turn + 1 < ADAM:
            current = following
            predict = dot(
                hidden_all[1].reshape(hidden_width, 128),
                current[...].reshape(hidden_width, 512),
                0,
                0,
            )
    own_all.wait_send()
    far_all.wait_send()


def keep(sources, targets, sem):
    copies = [
        pltpu.make_async_copy(source, target, sem.at[i])
        for i, (source, target) in enumerate(zip(sources, targets))
    ]
    for copy in copies:
        copy.start()
    for copy in copies:
        copy.wait()


def store(*refs):
    count = len(refs) // 2
    keep(refs[:count], refs[count : 2 * count], refs[-1])


def shards(
    initial,
    react_rates,
    snap_times,
    field_code,
    time_code,
    batch_ids,
    in_weight,
    in_moment,
    in_second,
    out_weight,
    out_moment,
    out_second,
):
    strips = lax.axis_size("strip")
    fields_dev = initial.shape[0]
    hidden_width = in_weight.shape[0]
    points = out_weight.shape[1]
    vmem = pl.BlockSpec(memory_space=pltpu.VMEM)
    hbm = pl.BlockSpec(memory_space=pltpu.HBM)
    dma = pltpu.SemaphoreType.DMA
    outs = pl.pallas_call(
        kernel,
        out_shape=(
            pltpu.VMEM(initial.shape, F32),
            pltpu.VMEM((strips, 8, in_weight.shape[1]), BF16),
            pltpu.VMEM(in_moment.shape, F32),
            pltpu.VMEM(in_second.shape, F32),
            pltpu.VMEM((4, hidden_width // 4, points), BF16),
            pltpu.VMEM(out_moment.shape, F32),
            pltpu.VMEM(out_second.shape, F32),
        ),
        in_specs=[hbm] * 12,
        out_specs=(vmem,) * 7,
        scratch_shapes=[
            pltpu.VMEM(initial.shape, F32),
            pltpu.SMEM(react_rates.shape, F32),
            pltpu.VMEM(snap_times.shape[::-1], jnp.int32),
            pltpu.VMEM(field_code.shape, BF16),
            pltpu.VMEM(time_code.shape, BF16),
            pltpu.VMEM(batch_ids.shape, jnp.int32),
            pltpu.VMEM((strips, 8, in_weight.shape[1]), BF16),
            pltpu.VMEM(in_moment.shape, F32),
            pltpu.VMEM(in_second.shape, F32),
            pltpu.VMEM((4, hidden_width // 4, points), BF16),
            pltpu.VMEM(out_moment.shape, F32),
            pltpu.VMEM(out_second.shape, F32),
            pltpu.VMEM((2, fields_dev, 2, 128), F32),
            pltpu.VMEM((2, fields_dev, 2, 128), F32),
            pltpu.VMEM((2 * fields_dev * 8, 128), F32),
            pltpu.VMEM((strips, 2, 128), BF16),
            pltpu.VMEM((4, strips, 2, 128), BF16),
            pltpu.VMEM((4, ADAM, 8, 128), F32),
            pltpu.VMEM((ADAM, 4, 4, 4, 8, 128), F32),
            pltpu.VMEM((ADAM, 16, 4, 8, 128), F32),
            pltpu.VMEM((ADAM, 4, 8, 128), F32),
            pltpu.VMEM((ADAM, 4, 8, 128), F32),
            pltpu.VMEM((8, 128), BF16),
            pltpu.VMEM((ADAM, strips, 8, 128), BF16),
            pltpu.VMEM((4, hidden_width // 4, points), BF16),
            dma((2,)),
            dma((2,)),
            dma((2,)),
            dma((1,)),
            dma((1,)),
            dma((1,)),
            dma((1,)),
            dma((3,)),
            dma((3,)),
            dma((ADAM,)),
            dma((ADAM,)),
            dma((ADAM,)),
            dma((ADAM,)),
            dma((1,)),
            dma((1,)),
            dma((ADAM, 3)),
            dma((ADAM, 3)),
            dma((2,)),
            dma((2,)),
            dma((12,)),
        ],
        compiler_params=pltpu.CompilerParams(
            collective_id=0, has_side_effects=True, vmem_limit_bytes=48 * 1024 * 1024
        ),
        name="ensemble",
    )(
        *(
            pltpu.with_memory_space_constraint(operand, pltpu.HBM)
            for operand in (
        initial,
        react_rates,
        jnp.transpose(snap_times),
        field_code,
        time_code,
        batch_ids,
        in_weight.reshape(strips, hidden_width // strips, in_weight.shape[1]),
        in_moment,
        in_second,
        out_weight.reshape(4, hidden_width // 4, points),
        out_moment,
        out_second,
            )
        )
    )
    outs = pl.pallas_call(
        store,
        out_shape=tuple(pltpu.HBM(out.shape, out.dtype) for out in outs),
        in_specs=[vmem] * 7,
        out_specs=(hbm,) * 7,
        scratch_shapes=[dma((7,))],
        name="store",
    )(*(pltpu.with_memory_space_constraint(out, pltpu.VMEM) for out in outs))
    fields, in_new, in_m, in_v, out_new, out_m, out_v = outs
    return (
        fields,
        in_new.reshape(in_weight.shape),
        in_m,
        in_v,
        out_new.reshape(out_weight.shape),
        out_m,
        out_v,
    )


def solution(mesh):
    in_specs = (
        P("group", "strip", None),
        P("group"),
        P(),
        P(),
        P(),
        P(None, "group"),
        P(),
        P("strip", None),
        P("strip", None),
        P(None, "strip"),
        P("group", "strip"),
        P("group", "strip"),
    )
    out_specs = (
        P("group", "strip", None),
        P(),
        P("strip", None),
        P("strip", None),
        P(None, "strip"),
        P("group", "strip"),
        P("group", "strip"),
    )
    return jax.shard_map(shards, mesh=mesh, in_specs=in_specs, out_specs=out_specs, check_vma=False)
```

```python
import functools

import jax
import jax.numpy as jnp
from jax import lax
from jax.experimental import pallas as pl
from jax.experimental.pallas import tpu as pltpu
from jax.sharding import PartitionSpec as P

STEPS = 2
SNAPS = 4
ADAM = 2
PRIOR = 100

DIFF_ROWS = 0.35
DIFF_COLS = 0.05
BETA_ONE = 0.9
BETA_TWO = 0.999
LEARN_RATE = 0.003
EPSILON = 1e-08
GELU_SCALE = 0.7978845608
GELU_CUBE = 0.044715

MESH = pl.DeviceIdType.MESH
F32 = jnp.float32
BF16 = jnp.bfloat16


def gelu_value(pre_act):
    return (
        0.5
        * pre_act
        * (1.0 + jnp.tanh(GELU_SCALE * (pre_act + GELU_CUBE * pre_act * pre_act * pre_act)))
    )


def gelu_slope(pre_act):
    tanh_part = jnp.tanh(GELU_SCALE * (pre_act + GELU_CUBE * pre_act * pre_act * pre_act))
    return 0.5 * (1.0 + tanh_part) + 0.5 * pre_act * (1.0 - tanh_part * tanh_part) * GELU_SCALE * (
        1.0 + 3.0 * GELU_CUBE * pre_act * pre_act
    )


def adam_update(weight, moment, second, gradient, step_count):
    moment = BETA_ONE * moment + (1.0 - BETA_ONE) * gradient
    second = BETA_TWO * second + (1.0 - BETA_TWO) * gradient * gradient
    update = (
        moment
        / (1.0 - BETA_ONE**step_count)
        / (jnp.sqrt(second / (1.0 - BETA_TWO**step_count)) + EPSILON)
    )
    return ((weight.astype(F32) - LEARN_RATE * update).astype(BF16), moment, second)


def dot(left, right, left_dim, right_dim):
    return lax.dot_general(
        left, right, (((left_dim,), (right_dim,)), ((), ())), preferred_element_type=F32
    )


def three_parts(value):
    high = value.astype(BF16)
    rest = value - high.astype(F32)
    middle = rest.astype(BF16)
    low = (rest - middle.astype(F32)).astype(BF16)
    return high, middle, low


def kernel(
    initial_hbm,
    rates_hbm,
    times_hbm,
    field_code_hbm,
    time_code_hbm,
    batch_ids_hbm,
    in_weight_hbm,
    in_moment_hbm,
    in_second_hbm,
    out_weight_hbm,
    out_moment_hbm,
    out_second_hbm,
    fields_out,
    in_weight_new,
    in_moment_new,
    in_second_new,
    out_weight_new,
    out_moment_new,
    out_second_new,
    initial,
    rates,
    times,
    field_code,
    time_code,
    batch_ids,
    in_weight,
    in_moment,
    in_second,
    out_weight,
    out_moment,
    out_second,
    edges,
    halo,
    states,
    pieces,
    arrived,
    counts,
    terms,
    plane_in,
    line_out,
    line_in,
    hidden_own,
    hidden_all,
    weight_mid,
    halo_send,
    halo_recv,
    piece_send,
    own_recv,
    far_recv,
    pool_send,
    pool_recv,
    count_send,
    count_recv,
    plane_send,
    plane_recv,
    line_send,
    line_recv,
    hidden_send,
    hidden_recv,
    weight_send,
    weight_recv,
    row_send,
    row_recv,
    load_sem,
    swap_send,
    swap_recv,
    plane_in_kernel,
):
    strips = lax.axis_size("strip")
    me = lax.axis_index("strip")
    g = lax.axis_index("group")
    far = lax.rem(g + 2, 4)
    mate = g + 1 - 2 * lax.rem(g, 2)
    far_mate = lax.rem(mate + 2, 4)
    fields = initial.shape[0]
    others = strips - 1
    at_y, at_z, at_x = me // 16, lax.rem(me // 4, 4), lax.rem(me, 4)

    def each(count, body):
        width = 7 if count % 7 == 0 else 1

        def steps(k, carry):
            for i in range(width):
                body(width * k + i)
            return carry

        lax.fori_loop(0, count // width, steps, 0)

    def other(k):
        return lax.rem(me + 1 + k, strips)

    def send(source, target, send_sem, recv_sem, strip, group):
        copy = pltpu.make_async_remote_copy(
            src_ref=source,
            dst_ref=target,
            send_sem=send_sem,
            recv_sem=recv_sem,
            device_id={"strip": strip, "group": group},
            device_id_type=MESH,
        )
        copy.start()
        return copy

    loads = [
        pltpu.make_async_copy(source, target, load_sem.at[i])
        for i, (source, target) in enumerate(
            (
                (initial_hbm, initial),
                (batch_ids_hbm, batch_ids),
                (times_hbm, times),
                (field_code_hbm, field_code),
                (time_code_hbm, time_code),
                (in_weight_hbm, in_weight),
                (rates_hbm, rates),
                (out_weight_hbm, out_weight),
                (in_moment_hbm, in_moment),
                (in_second_hbm, in_second),
                (out_moment_hbm, out_moment),
                (out_second_hbm, out_second),
            )
        )
    ]
    for load in loads:
        load.start()

    barrier = pltpu.get_barrier_semaphore()

    def greet(strip, group):
        pl.semaphore_signal(
            barrier, inc=1, device_id={"strip": strip, "group": group}, device_id_type=MESH
        )

    plane_peers = []
    line_peers = []
    for i in range(1, 16):
        ty, tx = lax.rem(at_y + i // 4, 4), lax.rem(at_x + i % 4, 4)
        plane_peers.append((16 * ty + 4 * at_z + tx, g))
    for i in range(1, 4):
        strip = 16 * at_y + 4 * lax.rem(at_z + i, 4) + at_x
        line_peers += [(strip, far), (strip, g)]
    line_peers.append((me, far))
    up = lax.rem(me + others, strips)
    down = lax.rem(me + 1, strips)
    for strip, group in [(up, g), (down, g)] + line_peers + plane_peers + [(me, mate), (me, far_mate)]:
        greet(strip, group)
    greeted = 26

    for load in loads[:3]:
        load.wait()
    edges[0] = initial[:, 0:2, :]
    edges[1] = initial[:, 2:4, :]

    kind_row = lax.broadcasted_iota(jnp.int32, (128, 128), 0)
    field_row = 16 * (kind_row // 32) + lax.rem(kind_row, 16)
    kind_lane = lax.broadcasted_iota(jnp.int32, (64, 128), 1)
    field_lane = 16 * (kind_lane // 32) + lax.rem(kind_lane, 16)
    spread = (lax.broadcasted_iota(jnp.int32, (64, 128), 0) == field_lane).astype(F32).astype(BF16)
    kind_times = dot(times[...].astype(F32).astype(BF16), spread, 1, 0)
    slot = lax.broadcasted_iota(jnp.int32, (4, 128), 0)
    own_time = jnp.sum(jnp.where(slot == g, kind_times, 0.0), axis=0, keepdims=True)
    step_lane = (lax.rem(lax.broadcasted_iota(jnp.int32, (1, 128), 1) // 16, 2) + 1).astype(F32)
    time_fits = jnp.where(own_time == step_lane, 1.0, 0.0)
    ones = jnp.ones((8, 128), BF16)
    for turn in range(ADAM):
        hits = (batch_ids[turn : turn + 1, :] == field_row).astype(F32).astype(BF16)
        counts[0, turn] = dot(ones, hits, 1, 1) * time_fits

    for load in loads[3:6]:
        load.wait()
    code_parts = []
    for part in range(4):
        for step in range(STEPS):
            code_parts.append(
                (
                    field_code[16 * part : 16 * part + 16, :].astype(F32)
                    + time_code[step : step + 1, :].astype(F32)
                ).astype(BF16)
            )
    code = jnp.concatenate(code_parts, axis=0)
    hidden_width = 8 * strips
    pre_act = dot(in_weight[...].reshape(hidden_width, 512), code, 1, 1)
    hidden = gelu_value(pre_act).astype(BF16)
    hidden_all[0] = hidden.reshape(strips, 8, 128)

    pl.semaphore_wait(barrier, greeted)

    halo_copies = [
        send(edges.at[0], halo.at[1], halo_send.at[0], halo_recv.at[1], up, g),
        send(edges.at[1], halo.at[0], halo_send.at[1], halo_recv.at[0], down, g),
    ]
    count_copies = [
        send(counts.at[0], counts.at[1 + i], count_send.at[i], count_recv.at[i], me, group)
        for i, group in enumerate((far, mate, far_mate))
    ]

    for load in loads[6:]:
        load.wait()
    for strip, group in line_peers:
        pl.semaphore_signal(
            plane_in_kernel,
            inc=1,
            device_id={"strip": strip, "group": group},
            device_id_type=MESH,
        )
    old_weight = out_weight[...].reshape(hidden_width, 512)
    predict = dot(hidden, old_weight, 0, 0)
    own_pre = dot(in_weight[me], code, 1, 1)

    for copy in halo_copies:
        copy.wait()

    row = lax.broadcasted_iota(jnp.int32, (8, 128), 0) + 4 * me - 2
    inside = jnp.logical_and(row >= 0, row < 4 * strips)

    def advance(center, rate):
        across = pltpu.roll(center, 1, 1) + pltpu.roll(center, 127, 1)
        return (
            center
            + DIFF_ROWS * (pltpu.roll(center, 1, 0) + pltpu.roll(center, 7, 0) - 2.0 * center)
            + DIFF_COLS * (across - 2.0 * center)
            + rate * center * (1.0 - center * center)
        )

    for field in range(fields):
        start = jnp.concatenate([halo[0, field], initial[field], halo[1, field]], axis=0)
        start = jnp.where(inside, start, 0.0)
        first = jnp.where(inside, advance(start, rates[field]), 0.0)
        second = advance(first, rates[field])
        states[8 * field : 8 * field + 8, :] = first
        states[8 * (fields + field) : 8 * (fields + field) + 8, :] = second
        fields_out[field] = second[2:6, :]

    def grid(shape):
        return (lax.broadcasted_iota(jnp.int32, shape, i) for i in range(2))

    def one_hot(hit):
        return jnp.where(hit, 1.0, 0.0).astype(BF16)

    kind_at, lane_at = grid((32, 128))
    repeat = one_hot(kind_at == lax.rem(lane_at, 32))
    point_at, lane_at = grid((128, 128))
    own_lanes = lax.rem(point_at, 4) == lane_at // 32
    four_at, point_at = grid((32, 128))
    fold = one_hot(four_at == point_at // 4)
    for line in range(4):
        chosen = states[pl.ds(2 + line, 32, stride=8), :].astype(BF16)
        spread_out = jnp.where(own_lanes, dot(chosen, repeat, 0, 0), 0.0).astype(BF16)
        piece = dot(fold, spread_out, 1, 0)
        pieces[16 * line : 16 * line + 16] = piece.reshape(16, 2, 128).astype(BF16)

    pl.semaphore_wait(plane_in_kernel, 7)
    def send_piece(k):
        t = other(k)
        send(pieces.at[t], arrived.at[0, me], piece_send.at[0], own_recv.at[0], t, g)
        send(pieces.at[t], arrived.at[1, me], piece_send.at[1], far_recv.at[0], t, far)

    each(others, send_piece)
    send(pieces.at[me], arrived.at[1, me], piece_send.at[1], far_recv.at[0], me, far)
    arrived[0, me] = pieces[me]

    def whole(source, target, send_sem, recv_sem):
        return pltpu.make_async_remote_copy(
            src_ref=source,
            dst_ref=target,
            send_sem=send_sem,
            recv_sem=recv_sem,
            device_id={"strip": me, "group": far},
            device_id_type=MESH,
        )

    most = pl.ds(0, others)
    own_all = whole(pieces.at[most], arrived.at[0, most], piece_send.at[0], own_recv.at[0])
    far_all = whole(pieces, arrived.at[1], piece_send.at[1], far_recv.at[0])
    own_all.wait_recv()
    far_all.wait_recv()
    pool_copy = send(
        arrived.at[pl.ds(0, 2)], arrived.at[pl.ds(2, 2)], pool_send.at[0], pool_recv.at[0], me, mate
    )
    for copy in count_copies:
        copy.wait()
    count = jnp.sum(counts[...], axis=0)
    point_at, row_at = grid((8 * strips, 2 * strips))
    unfold = one_hot(point_at // 4 == row_at)
    point_at, lane_at = grid((8 * strips, 128))
    lane_at2 = lax.broadcasted_iota(jnp.int32, (8 * strips, 256), 1)
    own_lanes = lax.rem(lax.broadcasted_iota(jnp.int32, (8 * strips, 256), 0), 4) == (
        lax.rem(lane_at2, 128) // 32
    )
    lane_at, kind_at = grid((256, 128))

    def pool_of(part, group, other_group):
        rows = [
            arrived[part + i].astype(F32).reshape(2 * strips, 128).astype(BF16) for i in range(2)
        ]
        points = dot(unfold, jnp.concatenate(rows, axis=1), 1, 0)
        points = jnp.where(own_lanes, points, 0.0).astype(BF16)
        start = jnp.where(lane_at < 128, 32 * group, 32 * other_group)
        return dot(one_hot(kind_at == start + lax.rem(lane_at, 32)), points, 0, 1)

    pool = pool_of(0, g, far)
    pool_copy.wait()
    pool = pool + pool_of(2, mate, far_mate)

    moment, second_moment = out_moment[...], out_second[...]
    row_weight, row_moment, row_second = in_weight[me], in_moment[...], in_second[...]
    current = out_weight
    for turn in range(ADAM):
        step_count = PRIOR + turn + 1
        number = count[turn, 0:1, :]
        delta = ((predict - pool) * (1.0 / 512.0)).astype(BF16)
        weights = current[...].reshape(hidden_width, 512)

        own_hidden = hidden_all[turn, pl.ds(g * (strips // 4), strips // 4)].reshape(
            hidden_width // 4, 128
        )
        grad = sum(dot(part, delta, 1, 0) for part in three_parts(own_hidden.astype(F32) * number))
        new_rows, moment, second_moment = adam_update(
            current[g], moment, second_moment, grad, step_count
        )
        following = weight_mid if turn + 1 < ADAM else out_weight_new
        following[g] = new_rows

        def weight_copy(part, i, group):
            return send(
                following.at[part],
                following.at[part],
                weight_send.at[turn, i],
                weight_recv.at[turn, i],
                me,
                group,
            )

        def start_weight():
            return [weight_copy(g, 0, far), weight_copy(g, 1, mate)]

        weight_copies = start_weight()
        terms[turn] = dot(weights, delta, 1, 1).reshape(4, 4, 4, 8, 128)

        def send_terms(k):
            ty = lax.rem(at_y + (k + 1) // 4, 4)
            tx = lax.rem(at_x + lax.rem(k + 1, 4), 4)
            send(
                terms.at[turn, ty, :, tx],
                plane_in.at[turn, 4 * at_y + at_x],
                plane_send.at[turn],
                plane_recv.at[turn],
                16 * ty + 4 * at_z + tx,
                g,
            )

        each(15, send_terms)
        plane_in[turn, 4 * at_y + at_x] = terms[turn, at_y, :, at_x]
        plane = plane_in.at[turn, pl.ds(0, 15)]
        plane_all = whole(plane, plane, plane_send.at[turn], plane_recv.at[turn])
        plane_all.wait_recv()
        line_out[turn] = jnp.sum(plane_in[turn], axis=0)

        def send_line(k):
            tz = lax.rem(at_z + k + 1, 4)
            send(
                line_out.at[turn, tz],
                line_in.at[turn, at_z],
                line_send.at[turn],
                line_recv.at[turn],
                16 * at_y + 4 * tz + at_x,
                g,
            )

        each(3, send_line)
        line_in[turn, at_z] = line_out[turn, at_z]
        line = line_in.at[turn, pl.ds(0, 3)]
        line_all = whole(line, line, line_send.at[turn], line_recv.at[turn])
        line_all.wait_recv()

        hidden_grad = jnp.sum(line_in[turn], axis=0)
        pre_grad = (hidden_grad * gelu_slope(own_pre)).astype(BF16)
        in_grad = sum(dot(part, code, 1, 0) for part in three_parts(pre_grad.astype(F32) * number))
        row_weight, row_moment, row_second = adam_update(
            row_weight, row_moment, row_second, in_grad, step_count
        )
        if turn + 1 < ADAM:
            own_pre = dot(row_weight, code, 1, 1)
            hidden_own[...] = gelu_value(own_pre).astype(BF16)
            hidden_all[1, me] = hidden_own[...]
            source, target, several = hidden_own, hidden_all.at[1, me], hidden_all.at[1, most]
            send_sem, recv_sem = hidden_send, hidden_recv
        else:
            half = pl.ds(pl.multiple_of(256 * lax.rem(g, 2), 256), 256)
            in_weight_new[me, :, half] = jnp.where(
                lax.rem(g, 2) == 0,
                row_weight[:, :256].astype(F32),
                row_weight[:, 256:].astype(F32),
            ).astype(BF16)
            source = target = in_weight_new.at[me, :, half]
            several = in_weight_new.at[most, :, half]
            send_sem, recv_sem = row_send, row_recv


        def send_rows(k):
            t = other(k)
            send(source, target, send_sem.at[0], recv_sem.at[at_y if turn + 1 == ADAM else 0], t, g)

        each(others, send_rows)
        if turn + 1 == ADAM:
            in_moment_new[...] = row_moment
            in_second_new[...] = row_second
            out_moment_new[...] = moment
            out_second_new[...] = second_moment
        weight_copies[0].wait()
        weight_copies.append(weight_copy(far, 2, mate))
        if turn + 1 == ADAM:
            swaps = []
            for i, step in enumerate((0, 1, 3, 2)):
                ty = lax.rem(at_y + step, 4)
                some = in_weight_new.at[pl.ds(16 * ty, 15 if step == 0 else 16), :, half]
                whole(some, some, send_sem.at[0], recv_sem.at[ty]).wait_recv()
                some = in_weight_new.at[pl.ds(16 * ty, 16), :, half]
                swaps.append(send(some, some, swap_send.at[i], swap_recv.at[i], me, mate))
            for swap in swaps:
                swap.wait()
            whole(several, several, send_sem.at[0], recv_sem.at[0]).wait_send()
        else:
            whole(several, several, send_sem.at[0], recv_sem.at[0]).wait()
        for copy in weight_copies[1:]:
            copy.wait()
        plane_all.wait_send()
        line_all.wait_send()
        if turn + 1 < ADAM:
            current = following
            predict = dot(
                hidden_all[1].reshape(hidden_width, 128),
                current[...].reshape(hidden_width, 512),
                0,
                0,
            )
    own_all.wait_send()
    far_all.wait_send()


def keep(sources, targets, sem):
    copies = [
        pltpu.make_async_copy(source, target, sem.at[i])
        for i, (source, target) in enumerate(zip(sources, targets))
    ]
    for copy in copies:
        copy.start()
    for copy in copies:
        copy.wait()


def store(*refs):
    count = len(refs) // 2
    keep(refs[:count], refs[count : 2 * count], refs[-1])


def shards(
    initial,
    react_rates,
    snap_times,
    field_code,
    time_code,
    batch_ids,
    in_weight,
    in_moment,
    in_second,
    out_weight,
    out_moment,
    out_second,
):
    strips = lax.axis_size("strip")
    fields_dev = initial.shape[0]
    hidden_width = in_weight.shape[0]
    points = out_weight.shape[1]
    vmem = pl.BlockSpec(memory_space=pltpu.VMEM)
    hbm = pl.BlockSpec(memory_space=pltpu.HBM)
    dma = pltpu.SemaphoreType.DMA
    outs = pl.pallas_call(
        kernel,
        out_shape=(
            pltpu.VMEM(initial.shape, F32),
            pltpu.VMEM((strips, 8, in_weight.shape[1]), BF16),
            pltpu.VMEM(in_moment.shape, F32),
            pltpu.VMEM(in_second.shape, F32),
            pltpu.VMEM((4, hidden_width // 4, points), BF16),
            pltpu.VMEM(out_moment.shape, F32),
            pltpu.VMEM(out_second.shape, F32),
        ),
        in_specs=[hbm] * 12,
        out_specs=(vmem,) * 7,
        scratch_shapes=[
            pltpu.VMEM(initial.shape, F32),
            pltpu.SMEM(react_rates.shape, F32),
            pltpu.VMEM(snap_times.shape[::-1], jnp.int32),
            pltpu.VMEM(field_code.shape, BF16),
            pltpu.VMEM(time_code.shape, BF16),
            pltpu.VMEM(batch_ids.shape, jnp.int32),
            pltpu.VMEM((strips, 8, in_weight.shape[1]), BF16),
            pltpu.VMEM(in_moment.shape, F32),
            pltpu.VMEM(in_second.shape, F32),
            pltpu.VMEM((4, hidden_width // 4, points), BF16),
            pltpu.VMEM(out_moment.shape, F32),
            pltpu.VMEM(out_second.shape, F32),
            pltpu.VMEM((2, fields_dev, 2, 128), F32),
            pltpu.VMEM((2, fields_dev, 2, 128), F32),
            pltpu.VMEM((2 * fields_dev * 8, 128), F32),
            pltpu.VMEM((strips, 2, 128), BF16),
            pltpu.VMEM((4, strips, 2, 128), BF16),
            pltpu.VMEM((4, ADAM, 8, 128), F32),
            pltpu.VMEM((ADAM, 4, 4, 4, 8, 128), F32),
            pltpu.VMEM((ADAM, 16, 4, 8, 128), F32),
            pltpu.VMEM((ADAM, 4, 8, 128), F32),
            pltpu.VMEM((ADAM, 4, 8, 128), F32),
            pltpu.VMEM((8, 128), BF16),
            pltpu.VMEM((ADAM, strips, 8, 128), BF16),
            pltpu.VMEM((4, hidden_width // 4, points), BF16),
            dma((2,)),
            dma((2,)),
            dma((2,)),
            dma((1,)),
            dma((1,)),
            dma((1,)),
            dma((1,)),
            dma((3,)),
            dma((3,)),
            dma((ADAM,)),
            dma((ADAM,)),
            dma((ADAM,)),
            dma((ADAM,)),
            dma((1,)),
            dma((1,)),
            dma((ADAM, 3)),
            dma((ADAM, 3)),
            dma((1,)),
            dma((4,)),
            dma((12,)),
            dma((4,)),
            dma((4,)),
            pltpu.SemaphoreType.REGULAR,
        ],
        compiler_params=pltpu.CompilerParams(
            collective_id=0, has_side_effects=True, vmem_limit_bytes=48 * 1024 * 1024
        ),
        name="ensemble",
    )(
        *(
            pltpu.with_memory_space_constraint(operand, pltpu.HBM)
            for operand in (
        initial,
        react_rates,
        jnp.transpose(snap_times),
        field_code,
        time_code,
        batch_ids,
        in_weight.reshape(strips, hidden_width // strips, in_weight.shape[1]),
        in_moment,
        in_second,
        out_weight.reshape(4, hidden_width // 4, points),
        out_moment,
        out_second,
            )
        )
    )
    outs = pl.pallas_call(
        store,
        out_shape=tuple(pltpu.HBM(out.shape, out.dtype) for out in outs),
        in_specs=[vmem] * 7,
        out_specs=(hbm,) * 7,
        scratch_shapes=[dma((7,))],
        name="store",
    )(*(pltpu.with_memory_space_constraint(out, pltpu.VMEM) for out in outs))
    fields, in_new, in_m, in_v, out_new, out_m, out_v = outs
    return (
        fields,
        in_new.reshape(in_weight.shape),
        in_m,
        in_v,
        out_new.reshape(out_weight.shape),
        out_m,
        out_v,
    )


def solution(mesh):
    in_specs = (
        P("group", "strip", None),
        P("group"),
        P(),
        P(),
        P(),
        P(None, "group"),
        P(),
        P("strip", None),
        P("strip", None),
        P(None, "strip"),
        P("group", "strip"),
        P("group", "strip"),
    )
    out_specs = (
        P("group", "strip", None),
        P(),
        P("strip", None),
        P("strip", None),
        P(None, "strip"),
        P("group", "strip"),
        P("group", "strip"),
    )
    return jax.shard_map(shards, mesh=mesh, in_specs=in_specs, out_specs=out_specs, check_vma=False)
```

```python
import functools

import jax
import jax.numpy as jnp
from jax import lax
from jax.experimental import pallas as pl
from jax.experimental.pallas import tpu as pltpu
from jax.sharding import PartitionSpec as P

STEPS = 2
SNAPS = 4
ADAM = 2
PRIOR = 100

DIFF_ROWS = 0.35
DIFF_COLS = 0.05
BETA_ONE = 0.9
BETA_TWO = 0.999
LEARN_RATE = 0.003
EPSILON = 1e-08
GELU_SCALE = 0.7978845608
GELU_CUBE = 0.044715

MESH = pl.DeviceIdType.MESH
F32 = jnp.float32
BF16 = jnp.bfloat16


def gelu_value(pre_act):
    return (
        0.5
        * pre_act
        * (1.0 + jnp.tanh(GELU_SCALE * (pre_act + GELU_CUBE * pre_act * pre_act * pre_act)))
    )


def gelu_slope(pre_act):
    tanh_part = jnp.tanh(GELU_SCALE * (pre_act + GELU_CUBE * pre_act * pre_act * pre_act))
    return 0.5 * (1.0 + tanh_part) + 0.5 * pre_act * (1.0 - tanh_part * tanh_part) * GELU_SCALE * (
        1.0 + 3.0 * GELU_CUBE * pre_act * pre_act
    )


def adam_update(weight, moment, second, gradient, step_count):
    moment = BETA_ONE * moment + (1.0 - BETA_ONE) * gradient
    second = BETA_TWO * second + (1.0 - BETA_TWO) * gradient * gradient
    update = (
        moment
        / (1.0 - BETA_ONE**step_count)
        / (jnp.sqrt(second / (1.0 - BETA_TWO**step_count)) + EPSILON)
    )
    return ((weight.astype(F32) - LEARN_RATE * update).astype(BF16), moment, second)


def dot(left, right, left_dim, right_dim):
    return lax.dot_general(
        left, right, (((left_dim,), (right_dim,)), ((), ())), preferred_element_type=F32
    )


def three_parts(value):
    high = value.astype(BF16)
    rest = value - high.astype(F32)
    middle = rest.astype(BF16)
    low = (rest - middle.astype(F32)).astype(BF16)
    return high, middle, low


def kernel(
    initial_hbm,
    rates_hbm,
    times_hbm,
    field_code_hbm,
    time_code_hbm,
    batch_ids_hbm,
    in_weight_hbm,
    in_moment_hbm,
    in_second_hbm,
    out_weight_hbm,
    out_moment_hbm,
    out_second_hbm,
    fields_out,
    in_weight_new,
    in_moment_new,
    in_second_new,
    out_weight_new,
    out_moment_new,
    out_second_new,
    initial,
    rates,
    times,
    field_code,
    time_code,
    batch_ids,
    in_weight,
    in_moment,
    in_second,
    out_weight,
    out_moment,
    out_second,
    edges,
    halo,
    states,
    pieces,
    arrived,
    counts,
    terms,
    plane_in,
    line_out,
    line_in,
    hidden_own,
    hidden_all,
    weight_mid,
    halo_send,
    halo_recv,
    piece_send,
    own_recv,
    far_recv,
    pool_send,
    pool_recv,
    count_send,
    count_recv,
    plane_send,
    plane_recv,
    line_send,
    line_recv,
    hidden_send,
    hidden_recv,
    weight_send,
    weight_recv,
    row_send,
    row_recv,
    load_sem,
    swap_send,
    swap_recv,
    plane_in_kernel,
):
    strips = lax.axis_size("strip")
    me = lax.axis_index("strip")
    g = lax.axis_index("group")
    far = lax.rem(g + 2, 4)
    mate = g + 1 - 2 * lax.rem(g, 2)
    far_mate = lax.rem(mate + 2, 4)
    fields = initial.shape[0]
    others = strips - 1
    core = lax.rem(g, 2)
    at_y, at_z, at_x = me // 16, lax.rem(me // 4, 4), lax.rem(me, 4)

    def each(count, body):
        width = 7 if count % 7 == 0 else 1

        def steps(k, carry):
            for i in range(width):
                body(width * k + i)
            return carry

        lax.fori_loop(0, count // width, steps, 0)

    def other(k):
        return lax.rem(me + 1 + k, strips)

    def send(source, target, send_sem, recv_sem, strip, group):
        copy = pltpu.make_async_remote_copy(
            src_ref=source,
            dst_ref=target,
            send_sem=send_sem,
            recv_sem=recv_sem,
            device_id={"strip": strip, "group": group},
            device_id_type=MESH,
        )
        copy.start()
        return copy

    loads = [
        pltpu.make_async_copy(source, target, load_sem.at[i])
        for i, (source, target) in enumerate(
            (
                (initial_hbm, initial),
                (batch_ids_hbm, batch_ids),
                (times_hbm, times),
                (field_code_hbm, field_code),
                (time_code_hbm, time_code),
                (in_weight_hbm, in_weight),
                (rates_hbm, rates),
                (out_weight_hbm, out_weight),
                (in_moment_hbm, in_moment),
                (in_second_hbm, in_second),
                (out_moment_hbm, out_moment),
                (out_second_hbm, out_second),
            )
        )
    ]
    for load in loads:
        load.start()

    barrier = pltpu.get_barrier_semaphore()

    def greet(strip, group):
        pl.semaphore_signal(
            barrier, inc=1, device_id={"strip": strip, "group": group}, device_id_type=MESH
        )

    plane_peers = []
    line_peers = []
    for i in range(1, 16):
        ty, tx = lax.rem(at_y + i // 4, 4), lax.rem(at_x + i % 4, 4)
        plane_peers.append((16 * ty + 4 * at_z + tx, g))
    for i in range(1, 4):
        strip = 16 * at_y + 4 * lax.rem(at_z + i, 4) + at_x
        line_peers += [(strip, far), (strip, g)]
    line_peers.append((me, far))
    up = lax.rem(me + others, strips)
    down = lax.rem(me + 1, strips)
    for strip, group in [(up, g), (down, g)] + line_peers + plane_peers + [(me, mate), (me, far_mate)]:
        greet(strip, group)
    greeted = 26

    for load in loads[:3]:
        load.wait()
    edges[0] = initial[:, 0:2, :]
    edges[1] = initial[:, 2:4, :]

    kind_row = lax.broadcasted_iota(jnp.int32, (128, 128), 0)
    field_row = 16 * (kind_row // 32) + lax.rem(kind_row, 16)
    kind_lane = lax.broadcasted_iota(jnp.int32, (64, 128), 1)
    field_lane = 16 * (kind_lane // 32) + lax.rem(kind_lane, 16)
    spread = (lax.broadcasted_iota(jnp.int32, (64, 128), 0) == field_lane).astype(F32).astype(BF16)
    kind_times = dot(times[...].astype(F32).astype(BF16), spread, 1, 0)
    slot = lax.broadcasted_iota(jnp.int32, (4, 128), 0)
    own_time = jnp.sum(jnp.where(slot == g, kind_times, 0.0), axis=0, keepdims=True)
    step_lane = (lax.rem(lax.broadcasted_iota(jnp.int32, (1, 128), 1) // 16, 2) + 1).astype(F32)
    time_fits = jnp.where(own_time == step_lane, 1.0, 0.0)
    ones = jnp.ones((8, 128), BF16)
    for turn in range(ADAM):
        hits = (batch_ids[turn : turn + 1, :] == field_row).astype(F32).astype(BF16)
        counts[0, turn] = dot(ones, hits, 1, 1) * time_fits

    for load in loads[3:6]:
        load.wait()
    code_parts = []
    for part in range(4):
        for step in range(STEPS):
            code_parts.append(
                (
                    field_code[16 * part : 16 * part + 16, :].astype(F32)
                    + time_code[step : step + 1, :].astype(F32)
                ).astype(BF16)
            )
    code = jnp.concatenate(code_parts, axis=0)
    hidden_width = 8 * strips
    pre_act = dot(in_weight[...].reshape(hidden_width, 512), code, 1, 1)
    hidden = gelu_value(pre_act).astype(BF16)
    hidden_all[0] = hidden.reshape(strips, 8, 128)

    pl.semaphore_wait(barrier, greeted)

    halo_copies = [
        send(edges.at[0], halo.at[1], halo_send.at[0], halo_recv.at[1], up, g),
        send(edges.at[1], halo.at[0], halo_send.at[1], halo_recv.at[0], down, g),
    ]
    count_copies = [
        send(counts.at[0], counts.at[1 + i], count_send.at[i], count_recv.at[i], me, group)
        for i, group in enumerate((far, mate, far_mate))
    ]

    for load in loads[6:]:
        load.wait()
    for strip, group in line_peers:
        pl.semaphore_signal(
            plane_in_kernel,
            inc=1,
            device_id={"strip": strip, "group": group},
            device_id_type=MESH,
        )
    old_weight = out_weight[...].reshape(hidden_width, 512)
    predict = dot(hidden, old_weight, 0, 0)
    own_pre = dot(in_weight[me], code, 1, 1)

    for copy in halo_copies:
        copy.wait()

    row = lax.broadcasted_iota(jnp.int32, (8, 128), 0) + 4 * me - 2
    inside = jnp.logical_and(row >= 0, row < 4 * strips)

    def advance(center, rate):
        across = pltpu.roll(center, 1, 1) + pltpu.roll(center, 127, 1)
        return (
            center
            + DIFF_ROWS * (pltpu.roll(center, 1, 0) + pltpu.roll(center, 7, 0) - 2.0 * center)
            + DIFF_COLS * (across - 2.0 * center)
            + rate * center * (1.0 - center * center)
        )

    for field in range(fields):
        start = jnp.concatenate([halo[0, field], initial[field], halo[1, field]], axis=0)
        start = jnp.where(inside, start, 0.0)
        first = jnp.where(inside, advance(start, rates[field]), 0.0)
        second = advance(first, rates[field])
        states[8 * field : 8 * field + 8, :] = first
        states[8 * (fields + field) : 8 * (fields + field) + 8, :] = second
        fields_out[field] = second[2:6, :]

    def grid(shape):
        return (lax.broadcasted_iota(jnp.int32, shape, i) for i in range(2))

    def one_hot(hit):
        return jnp.where(hit, 1.0, 0.0).astype(BF16)

    kind_at, lane_at = grid((32, 128))
    repeat = one_hot(kind_at == lax.rem(lane_at, 32))
    point_at, lane_at = grid((128, 128))
    own_lanes = lax.rem(point_at, 4) == lane_at // 32
    four_at, point_at = grid((32, 128))
    fold = one_hot(four_at == point_at // 4)
    for line in range(4):
        chosen = states[pl.ds(2 + line, 32, stride=8), :].astype(BF16)
        spread_out = jnp.where(own_lanes, dot(chosen, repeat, 0, 0), 0.0).astype(BF16)
        piece = dot(fold, spread_out, 1, 0)
        pieces[16 * line : 16 * line + 16] = piece.reshape(16, 2, 128).astype(BF16)

    pl.semaphore_wait(plane_in_kernel, 7)
    def send_piece(k):
        t = other(k)
        send(pieces.at[t], arrived.at[0, me], piece_send.at[0], own_recv.at[0], t, g)
        send(pieces.at[t], arrived.at[1, me], piece_send.at[1], far_recv.at[0], t, far)

    each(others, send_piece)
    send(pieces.at[me], arrived.at[1, me], piece_send.at[1], far_recv.at[0], me, far)
    arrived[0, me] = pieces[me]

    def whole(source, target, send_sem, recv_sem):
        return pltpu.make_async_remote_copy(
            src_ref=source,
            dst_ref=target,
            send_sem=send_sem,
            recv_sem=recv_sem,
            device_id={"strip": me, "group": far},
            device_id_type=MESH,
        )

    most = pl.ds(0, others)
    own_all = whole(pieces.at[most], arrived.at[0, most], piece_send.at[0], own_recv.at[0])
    far_all = whole(pieces, arrived.at[1], piece_send.at[1], far_recv.at[0])
    own_all.wait_recv()
    far_all.wait_recv()
    pool_copy = send(
        arrived.at[pl.ds(0, 2)], arrived.at[pl.ds(2, 2)], pool_send.at[0], pool_recv.at[0], me, mate
    )
    for copy in count_copies:
        copy.wait()
    count = jnp.sum(counts[...], axis=0)
    point_at, row_at = grid((8 * strips, 2 * strips))
    unfold = one_hot(point_at // 4 == row_at)
    point_at, lane_at = grid((8 * strips, 128))
    lane_at2 = lax.broadcasted_iota(jnp.int32, (8 * strips, 256), 1)
    own_lanes = lax.rem(lax.broadcasted_iota(jnp.int32, (8 * strips, 256), 0), 4) == (
        lax.rem(lane_at2, 128) // 32
    )
    lane_at, kind_at = grid((256, 128))

    def pool_of(part, group, other_group):
        rows = [
            arrived[part + i].astype(F32).reshape(2 * strips, 128).astype(BF16) for i in range(2)
        ]
        points = dot(unfold, jnp.concatenate(rows, axis=1), 1, 0)
        points = jnp.where(own_lanes, points, 0.0).astype(BF16)
        start = jnp.where(lane_at < 128, 32 * group, 32 * other_group)
        return dot(one_hot(kind_at == start + lax.rem(lane_at, 32)), points, 0, 1)

    pool = pool_of(0, g, far)
    pool_copy.wait()
    pool = pool + pool_of(2, mate, far_mate)

    moment, second_moment = out_moment[...], out_second[...]
    row_weight, row_moment, row_second = in_weight[me], in_moment[...], in_second[...]
    current = out_weight
    for turn in range(ADAM):
        step_count = PRIOR + turn + 1
        number = count[turn, 0:1, :]
        delta = ((predict - pool) * (1.0 / 512.0)).astype(BF16)
        weights = current[...].reshape(hidden_width, 512)

        terms[turn] = dot(weights, delta, 1, 1).reshape(4, 4, 4, 8, 128)

        def send_terms(k):
            ty = lax.rem(at_y + (k + 1) // 4, 4)
            tx = lax.rem(at_x + lax.rem(k + 1, 4), 4)
            send(
                terms.at[turn, ty, :, tx],
                plane_in.at[turn, 4 * at_y + at_x],
                plane_send.at[turn],
                plane_recv.at[turn],
                16 * ty + 4 * at_z + tx,
                g,
            )

        each(15, send_terms)
        plane_in[turn, 4 * at_y + at_x] = terms[turn, at_y, :, at_x]

        own_hidden = hidden_all[turn, pl.ds(g * (strips // 4), strips // 4)].reshape(
            hidden_width // 4, 128
        )
        grad = sum(dot(part, delta, 1, 0) for part in three_parts(own_hidden.astype(F32) * number))
        new_rows, moment, second_moment = adam_update(
            current[g], moment, second_moment, grad, step_count
        )
        following = weight_mid if turn + 1 < ADAM else out_weight_new
        following[g] = new_rows

        def weight_copy(part, i, group):
            return send(
                following.at[part],
                following.at[part],
                weight_send.at[turn, i],
                weight_recv.at[turn, i],
                me,
                group,
            )

        def start_weight():
            return [weight_copy(g, 0, far), weight_copy(g, 1, mate)]

        weight_copies = start_weight()
        slope = gelu_slope(own_pre)
        plane = plane_in.at[turn, pl.ds(0, 15)]
        plane_all = whole(plane, plane, plane_send.at[turn], plane_recv.at[turn])
        plane_all.wait_recv()
        line_out[turn] = jnp.sum(plane_in[turn], axis=0)

        def send_line(k):
            tz = lax.rem(at_z + k + 1, 4)
            send(
                line_out.at[turn, tz],
                line_in.at[turn, at_z],
                line_send.at[turn],
                line_recv.at[turn],
                16 * at_y + 4 * tz + at_x,
                g,
            )

        each(3, send_line)
        line_in[turn, at_z] = line_out[turn, at_z]
        line = line_in.at[turn, pl.ds(0, 3)]
        line_all = whole(line, line, line_send.at[turn], line_recv.at[turn])
        line_all.wait_recv()

        hidden_grad = jnp.sum(line_in[turn], axis=0)
        pre_grad = (hidden_grad * slope).astype(BF16)
        parts = [part.astype(F32) for part in three_parts(pre_grad.astype(F32) * number)]
        in_grads = dot(jnp.concatenate(parts, axis=0).astype(BF16), code, 1, 0)
        in_grad = in_grads[0:8] + in_grads[8:16] + in_grads[16:24]
        row_weight, row_moment, row_second = adam_update(
            row_weight, row_moment, row_second, in_grad, step_count
        )
        if turn + 1 < ADAM:
            own_pre = dot(row_weight, code, 1, 1)
            hidden_own[...] = gelu_value(own_pre).astype(BF16)
            hidden_all[1, me] = hidden_own[...]
            source, target, several = hidden_own, hidden_all.at[1, me], hidden_all.at[1, most]
            send_sem, recv_sem = hidden_send, hidden_recv
        else:
            in_weight_new[core, me] = jnp.where(
                core == 0, row_weight[:, :256].astype(F32), row_weight[:, 256:].astype(F32)
            ).astype(BF16)
            source = target = in_weight_new.at[core, me]
            several = in_weight_new.at[core, most]
            send_sem, recv_sem = row_send, row_recv


        def send_rows(k):
            t = other(k)
            send(source, target, send_sem.at[0], recv_sem.at[0], t, g)

        each(others, send_rows)
        if turn + 1 == ADAM:
            in_moment_new[...] = row_moment
            in_second_new[...] = row_second
            out_moment_new[...] = moment
            out_second_new[...] = second_moment
        weight_copies[0].wait()
        weight_copies.append(weight_copy(far, 2, mate))
        whole(several, several, send_sem.at[0], recv_sem.at[0]).wait()
        if turn + 1 == ADAM:
            columns = in_weight_new.at[core]
            send(columns, columns, swap_send.at[0], swap_recv.at[0], me, mate).wait()
        for copy in weight_copies[1:]:
            copy.wait()
        plane_all.wait_send()
        line_all.wait_send()
        if turn + 1 < ADAM:
            current = following
            predict = dot(
                hidden_all[1].reshape(hidden_width, 128),
                current[...].reshape(hidden_width, 512),
                0,
                0,
            )
    own_all.wait_send()
    far_all.wait_send()


def store(*refs):
    sources, targets, sem = refs[:7], refs[7:14], refs[14]
    width = sources[1].shape[-1]
    pairs = [(sources[1].at[i], targets[1].at[:, :, pl.ds(width * i, width)]) for i in range(2)]
    pairs += [(sources[i], targets[i]) for i in (4, 5, 6, 0, 2, 3)]
    copies = [
        pltpu.make_async_copy(source, target, sem.at[i]) for i, (source, target) in enumerate(pairs)
    ]
    for copy in copies:
        copy.start()
    for copy in copies:
        copy.wait()


def shards(
    initial,
    react_rates,
    snap_times,
    field_code,
    time_code,
    batch_ids,
    in_weight,
    in_moment,
    in_second,
    out_weight,
    out_moment,
    out_second,
):
    strips = lax.axis_size("strip")
    fields_dev = initial.shape[0]
    hidden_width = in_weight.shape[0]
    points = out_weight.shape[1]
    vmem = pl.BlockSpec(memory_space=pltpu.VMEM)
    hbm = pl.BlockSpec(memory_space=pltpu.HBM)
    dma = pltpu.SemaphoreType.DMA
    outs = pl.pallas_call(
        kernel,
        out_shape=(
            pltpu.VMEM(initial.shape, F32),
            pltpu.VMEM((2, strips, 8, in_weight.shape[1] // 2), BF16),
            pltpu.VMEM(in_moment.shape, F32),
            pltpu.VMEM(in_second.shape, F32),
            pltpu.VMEM((4, hidden_width // 4, points), BF16),
            pltpu.VMEM(out_moment.shape, F32),
            pltpu.VMEM(out_second.shape, F32),
        ),
        in_specs=[hbm] * 12,
        out_specs=(vmem,) * 7,
        scratch_shapes=[
            pltpu.VMEM(initial.shape, F32),
            pltpu.SMEM(react_rates.shape, F32),
            pltpu.VMEM(snap_times.shape[::-1], jnp.int32),
            pltpu.VMEM(field_code.shape, BF16),
            pltpu.VMEM(time_code.shape, BF16),
            pltpu.VMEM(batch_ids.shape, jnp.int32),
            pltpu.VMEM((strips, 8, in_weight.shape[1]), BF16),
            pltpu.VMEM(in_moment.shape, F32),
            pltpu.VMEM(in_second.shape, F32),
            pltpu.VMEM((4, hidden_width // 4, points), BF16),
            pltpu.VMEM(out_moment.shape, F32),
            pltpu.VMEM(out_second.shape, F32),
            pltpu.VMEM((2, fields_dev, 2, 128), F32),
            pltpu.VMEM((2, fields_dev, 2, 128), F32),
            pltpu.VMEM((2 * fields_dev * 8, 128), F32),
            pltpu.VMEM((strips, 2, 128), BF16),
            pltpu.VMEM((4, strips, 2, 128), BF16),
            pltpu.VMEM((4, ADAM, 8, 128), F32),
            pltpu.VMEM((ADAM, 4, 4, 4, 8, 128), F32),
            pltpu.VMEM((ADAM, 16, 4, 8, 128), F32),
            pltpu.VMEM((ADAM, 4, 8, 128), F32),
            pltpu.VMEM((ADAM, 4, 8, 128), F32),
            pltpu.VMEM((8, 128), BF16),
            pltpu.VMEM((ADAM, strips, 8, 128), BF16),
            pltpu.VMEM((4, hidden_width // 4, points), BF16),
            dma((2,)),
            dma((2,)),
            dma((2,)),
            dma((1,)),
            dma((1,)),
            dma((1,)),
            dma((1,)),
            dma((3,)),
            dma((3,)),
            dma((ADAM,)),
            dma((ADAM,)),
            dma((ADAM,)),
            dma((ADAM,)),
            dma((1,)),
            dma((1,)),
            dma((ADAM, 3)),
            dma((ADAM, 3)),
            dma((1,)),
            dma((1,)),
            dma((12,)),
            dma((1,)),
            dma((1,)),
            pltpu.SemaphoreType.REGULAR,
        ],
        compiler_params=pltpu.CompilerParams(
            collective_id=0, has_side_effects=True, vmem_limit_bytes=48 * 1024 * 1024
        ),
        name="ensemble",
    )(
        *(
            pltpu.with_memory_space_constraint(operand, pltpu.HBM)
            for operand in (
        initial,
        react_rates,
        jnp.transpose(snap_times),
        field_code,
        time_code,
        batch_ids,
        in_weight.reshape(strips, hidden_width // strips, in_weight.shape[1]),
        in_moment,
        in_second,
        out_weight.reshape(4, hidden_width // 4, points),
        out_moment,
        out_second,
            )
        )
    )
    outs = pl.pallas_call(
        store,
        out_shape=tuple(
            pltpu.HBM((strips, 8, in_weight.shape[1]) if i == 1 else out.shape, out.dtype)
            for i, out in enumerate(outs)
        ),
        in_specs=[vmem] * 7,
        out_specs=(hbm,) * 7,
        scratch_shapes=[dma((8,))],
        name="store",
    )(*(pltpu.with_memory_space_constraint(out, pltpu.VMEM) for out in outs))
    fields, in_new, in_m, in_v, out_new, out_m, out_v = outs
    return (
        fields,
        in_new.reshape(in_weight.shape),
        in_m,
        in_v,
        out_new.reshape(out_weight.shape),
        out_m,
        out_v,
    )


def solution(mesh):
    in_specs = (
        P("group", "strip", None),
        P("group"),
        P(),
        P(),
        P(),
        P(None, "group"),
        P(),
        P("strip", None),
        P("strip", None),
        P(None, "strip"),
        P("group", "strip"),
        P("group", "strip"),
    )
    out_specs = (
        P("group", "strip", None),
        P(),
        P("strip", None),
        P("strip", None),
        P(None, "strip"),
        P("group", "strip"),
        P("group", "strip"),
    )
    return jax.shard_map(shards, mesh=mesh, in_specs=in_specs, out_specs=out_specs, check_vma=False)
```

```python
import functools

import jax
import jax.numpy as jnp
from jax import lax
from jax.experimental import pallas as pl
from jax.experimental.pallas import tpu as pltpu
from jax.sharding import PartitionSpec as P

STEPS = 2
SNAPS = 4
ADAM = 2
PRIOR = 100

DIFF_ROWS = 0.35
DIFF_COLS = 0.05
BETA_ONE = 0.9
BETA_TWO = 0.999
LEARN_RATE = 0.003
EPSILON = 1e-08
GELU_SCALE = 0.7978845608
GELU_CUBE = 0.044715

MESH = pl.DeviceIdType.MESH
F32 = jnp.float32
BF16 = jnp.bfloat16

def gelu_value(pre_act):
    return (
        0.5
        * pre_act
        * (1.0 + jnp.tanh(GELU_SCALE * (pre_act + GELU_CUBE * pre_act * pre_act * pre_act)))
    )

def gelu_slope(pre_act):
    tanh_part = jnp.tanh(GELU_SCALE * (pre_act + GELU_CUBE * pre_act * pre_act * pre_act))
    return 0.5 * (1.0 + tanh_part) + 0.5 * pre_act * (1.0 - tanh_part * tanh_part) * GELU_SCALE * (
        1.0 + 3.0 * GELU_CUBE * pre_act * pre_act
    )

def adam_update(weight, moment, second, gradient, step_count):
    moment = BETA_ONE * moment + (1.0 - BETA_ONE) * gradient
    second = BETA_TWO * second + (1.0 - BETA_TWO) * gradient * gradient
    update = (
        moment
        / (1.0 - BETA_ONE**step_count)
        / (jnp.sqrt(second / (1.0 - BETA_TWO**step_count)) + EPSILON)
    )
    return ((weight.astype(F32) - LEARN_RATE * update).astype(BF16), moment, second)

def dot(left, right, left_dim, right_dim):
    return lax.dot_general(
        left, right, (((left_dim,), (right_dim,)), ((), ())), preferred_element_type=F32
    )

def three_parts(value):
    high = value.astype(BF16)
    rest = value - high.astype(F32)
    middle = rest.astype(BF16)
    low = (rest - middle.astype(F32)).astype(BF16)
    return high, middle, low

def kernel(
    initial_hbm,
    rates_hbm,
    times_hbm,
    field_code_hbm,
    time_code_hbm,
    batch_ids_hbm,
    in_weight_hbm,
    in_moment_hbm,
    in_second_hbm,
    out_weight_hbm,
    out_moment_hbm,
    out_second_hbm,
    fields_out,
    in_weight_new,
    in_moment_new,
    in_second_new,
    out_weight_new,
    out_moment_new,
    out_second_new,
    initial,
    rates,
    times,
    field_code,
    time_code,
    batch_ids,
    in_weight,
    in_moment,
    in_second,
    out_weight,
    out_moment,
    out_second,
    edges,
    halo,
    states,
    pieces,
    arrived,
    counts,
    terms,
    plane_in,
    line_out,
    line_in,
    hidden_own,
    hidden_all,
    weight_mid,
    halo_send,
    halo_recv,
    piece_send,
    own_recv,
    far_recv,
    pool_send,
    pool_recv,
    count_send,
    count_recv,
    plane_send,
    plane_recv,
    line_send,
    line_recv,
    hidden_send,
    hidden_recv,
    weight_send,
    weight_recv,
    row_send,
    row_recv,
    load_sem,
    swap_send,
    swap_recv,
    plane_in_kernel,
):
    strips = lax.axis_size("strip")
    me = lax.axis_index("strip")
    g = lax.axis_index("group")
    far = lax.rem(g + 2, 4)
    mate = g + 1 - 2 * lax.rem(g, 2)
    far_mate = lax.rem(mate + 2, 4)
    fields = initial.shape[0]
    others = strips - 1
    core = lax.rem(g, 2)
    at_y, at_z, at_x = me // 16, lax.rem(me // 4, 4), lax.rem(me, 4)

    def each(count, body):
        width = next(w for w in (7, 5, 3) if count % w == 0)

        def steps(k, carry):
            for i in range(width):
                body(width * k + i)
            return carry

        lax.fori_loop(0, count // width, steps, 0)

    def other(k):
        return lax.rem(me + 1 + k, strips)

    def send(source, target, send_sem, recv_sem, strip, group):
        copy = pltpu.make_async_remote_copy(
            src_ref=source,
            dst_ref=target,
            send_sem=send_sem,
            recv_sem=recv_sem,
            device_id={"strip": strip, "group": group},
            device_id_type=MESH,
        )
        copy.start()
        return copy

    loads = [
        pltpu.make_async_copy(source, target, load_sem.at[i])
        for i, (source, target) in enumerate(
            (
                (initial_hbm, initial),
                (batch_ids_hbm, batch_ids),
                (times_hbm, times),
                (field_code_hbm, field_code),
                (time_code_hbm, time_code),
                (in_weight_hbm, in_weight),
                (rates_hbm, rates),
                (out_weight_hbm, out_weight),
                (in_moment_hbm, in_moment),
                (in_second_hbm, in_second),
                (out_moment_hbm, out_moment),
                (out_second_hbm, out_second),
            )
        )
    ]
    for load in loads:
        load.start()

    barrier = pltpu.get_barrier_semaphore()

    def greet(strip, group):
        pl.semaphore_signal(
            barrier, inc=1, device_id={"strip": strip, "group": group}, device_id_type=MESH
        )

    plane_peers = []
    line_peers = []
    for i in range(1, 16):
        ty, tx = lax.rem(at_y + i // 4, 4), lax.rem(at_x + i % 4, 4)
        plane_peers.append((16 * ty + 4 * at_z + tx, g))
    for i in range(1, 4):
        strip = 16 * at_y + 4 * lax.rem(at_z + i, 4) + at_x
        line_peers += [(strip, far), (strip, g)]
    line_peers.append((me, far))
    up = lax.rem(me + others, strips)
    down = lax.rem(me + 1, strips)
    for strip, group in [(up, g), (down, g)] + line_peers + plane_peers + [(me, mate), (me, far_mate)]:
        greet(strip, group)
    greeted = 26

    loads[0].wait()
    edges[0] = initial[:, 0:2, :]
    edges[1] = initial[:, 2:4, :]

    pl.semaphore_wait(barrier, greeted)

    halo_copies = [
        send(edges.at[0], halo.at[1], halo_send.at[0], halo_recv.at[1], up, g),
        send(edges.at[1], halo.at[0], halo_send.at[1], halo_recv.at[0], down, g),
    ]
    for strip, group in line_peers:
        pl.semaphore_signal(
            plane_in_kernel,
            inc=1,
            device_id={"strip": strip, "group": group},
            device_id_type=MESH,
        )
    for load in loads[1:3]:
        load.wait()
    kind_row = lax.broadcasted_iota(jnp.int32, (128, 128), 0)
    field_row = 16 * (kind_row // 32) + lax.rem(kind_row, 16)
    kind_lane = lax.broadcasted_iota(jnp.int32, (64, 128), 1)
    field_lane = 16 * (kind_lane // 32) + lax.rem(kind_lane, 16)
    spread = (lax.broadcasted_iota(jnp.int32, (64, 128), 0) == field_lane).astype(F32).astype(BF16)
    kind_times = dot(times[...].astype(F32).astype(BF16), spread, 1, 0)
    slot = lax.broadcasted_iota(jnp.int32, (4, 128), 0)
    own_time = jnp.sum(jnp.where(slot == g, kind_times, 0.0), axis=0, keepdims=True)
    step_lane = (lax.rem(lax.broadcasted_iota(jnp.int32, (1, 128), 1) // 16, 2) + 1).astype(F32)
    time_fits = jnp.where(own_time == step_lane, 1.0, 0.0)
    ones = jnp.ones((8, 128), BF16)
    for turn in range(ADAM):
        hits = (batch_ids[turn : turn + 1, :] == field_row).astype(F32).astype(BF16)
        counts[0, turn] = dot(ones, hits, 1, 1) * time_fits

    count_copies = [
        send(counts.at[0], counts.at[1 + i], count_send.at[i], count_recv.at[i], me, group)
        for i, group in enumerate((far, mate, far_mate))
    ]

    for load in loads[6:]:
        load.wait()

    for load in loads[3:6]:
        load.wait()
    code_parts = []
    for part in range(4):
        for step in range(STEPS):
            code_parts.append(
                (
                    field_code[16 * part : 16 * part + 16, :].astype(F32)
                    + time_code[step : step + 1, :].astype(F32)
                ).astype(BF16)
            )
    code = jnp.concatenate(code_parts, axis=0)
    hidden_width = 8 * strips
    pre_act = dot(in_weight[...].reshape(hidden_width, 512), code, 1, 1)
    hidden = gelu_value(pre_act).astype(BF16)
    hidden_all[0] = hidden.reshape(strips, 8, 128)

    old_weight = out_weight[...].reshape(hidden_width, 512)
    predict = dot(hidden, old_weight, 0, 0)
    own_pre = dot(in_weight[me], code, 1, 1)

    for copy in halo_copies:
        copy.wait()

    row = lax.broadcasted_iota(jnp.int32, (8, 128), 0) + 4 * me - 2
    inside = jnp.logical_and(row >= 0, row < 4 * strips)

    def advance(center, rate):
        across = pltpu.roll(center, 1, 1) + pltpu.roll(center, 127, 1)
        return (
            center
            + DIFF_ROWS * (pltpu.roll(center, 1, 0) + pltpu.roll(center, 7, 0) - 2.0 * center)
            + DIFF_COLS * (across - 2.0 * center)
            + rate * center * (1.0 - center * center)
        )

    for field in range(fields):
        start = jnp.concatenate([halo[0, field], initial[field], halo[1, field]], axis=0)
        start = jnp.where(inside, start, 0.0)
        first = jnp.where(inside, advance(start, rates[field]), 0.0)
        second = advance(first, rates[field])
        states[8 * field : 8 * field + 8, :] = first
        states[8 * (fields + field) : 8 * (fields + field) + 8, :] = second
        fields_out[field] = second[2:6, :]

    def grid(shape):
        return (lax.broadcasted_iota(jnp.int32, shape, i) for i in range(2))

    def one_hot(hit):
        return jnp.where(hit, 1.0, 0.0).astype(BF16)

    kind_at, lane_at = grid((32, 128))
    repeat = one_hot(kind_at == lax.rem(lane_at, 32))
    point_at, lane_at = grid((128, 128))
    own_lanes = lax.rem(point_at, 4) == lane_at // 32
    four_at, point_at = grid((32, 128))
    fold = one_hot(four_at == point_at // 4)
    for line in range(4):
        chosen = states[pl.ds(2 + line, 32, stride=8), :].astype(BF16)
        spread_out = jnp.where(own_lanes, dot(chosen, repeat, 0, 0), 0.0).astype(BF16)
        piece = dot(fold, spread_out, 1, 0)
        pieces[16 * line : 16 * line + 16] = piece.reshape(16, 2, 128).astype(BF16)

    pl.semaphore_wait(plane_in_kernel, 7)
    def send_piece(k):
        t = other(k)
        send(pieces.at[t], arrived.at[0, me], piece_send.at[0], own_recv.at[0], t, g)
        send(pieces.at[t], arrived.at[1, me], piece_send.at[1], far_recv.at[0], t, far)

    each(others, send_piece)
    send(pieces.at[me], arrived.at[1, me], piece_send.at[1], far_recv.at[0], me, far)
    arrived[0, me] = pieces[me]

    def whole(source, target, send_sem, recv_sem):
        return pltpu.make_async_remote_copy(
            src_ref=source,
            dst_ref=target,
            send_sem=send_sem,
            recv_sem=recv_sem,
            device_id={"strip": me, "group": far},
            device_id_type=MESH,
        )

    most = pl.ds(0, others)
    own_all = whole(pieces.at[most], arrived.at[0, most], piece_send.at[0], own_recv.at[0])
    far_all = whole(pieces, arrived.at[1], piece_send.at[1], far_recv.at[0])
    own_all.wait_recv()
    far_all.wait_recv()
    pool_copy = send(
        arrived.at[pl.ds(0, 2)], arrived.at[pl.ds(2, 2)], pool_send.at[0], pool_recv.at[0], me, mate
    )
    for copy in count_copies:
        copy.wait()
    count = jnp.sum(counts[...], axis=0)
    point_at, row_at = grid((8 * strips, 2 * strips))
    unfold = one_hot(point_at // 4 == row_at)
    point_at, lane_at = grid((8 * strips, 128))
    lane_at2 = lax.broadcasted_iota(jnp.int32, (8 * strips, 256), 1)
    own_lanes = lax.rem(lax.broadcasted_iota(jnp.int32, (8 * strips, 256), 0), 4) == (
        lax.rem(lane_at2, 128) // 32
    )
    lane_at, kind_at = grid((256, 128))

    def pool_of(part, group, other_group):
        rows = [
            arrived[part + i].astype(F32).reshape(2 * strips, 128).astype(BF16) for i in range(2)
        ]
        points = dot(unfold, jnp.concatenate(rows, axis=1), 1, 0)
        points = jnp.where(own_lanes, points, 0.0).astype(BF16)
        start = jnp.where(lane_at < 128, 32 * group, 32 * other_group)
        return dot(one_hot(kind_at == start + lax.rem(lane_at, 32)), points, 0, 1)

    pool = pool_of(0, g, far)
    pool_copy.wait()
    pool = pool + pool_of(2, mate, far_mate)

    moment, second_moment = out_moment[...], out_second[...]
    row_weight, row_moment, row_second = in_weight[me], in_moment[...], in_second[...]
    current = out_weight
    for turn in range(ADAM):
        step_count = PRIOR + turn + 1
        number = count[turn, 0:1, :]
        delta = ((predict - pool) * (1.0 / 512.0)).astype(BF16)
        weights = current[...].reshape(hidden_width, 512)

        terms[turn] = dot(weights, delta, 1, 1).reshape(4, 4, 4, 8, 128)

        def send_terms(k):
            ty = lax.rem(at_y + (k + 1) // 4, 4)
            tx = lax.rem(at_x + lax.rem(k + 1, 4), 4)
            send(
                terms.at[turn, ty, :, tx],
                plane_in.at[turn, 4 * at_y + at_x],
                plane_send.at[turn],
                plane_recv.at[turn],
                16 * ty + 4 * at_z + tx,
                g,
            )

        each(15, send_terms)
        plane_in[turn, 4 * at_y + at_x] = terms[turn, at_y, :, at_x]

        own_hidden = hidden_all[turn, pl.ds(g * (strips // 4), strips // 4)].reshape(
            hidden_width // 4, 128
        )
        grad = sum(dot(part, delta, 1, 0) for part in three_parts(own_hidden.astype(F32) * number))
        new_rows, moment, second_moment = adam_update(
            current[g], moment, second_moment, grad, step_count
        )
        following = weight_mid if turn + 1 < ADAM else out_weight_new
        following[g] = new_rows

        def weight_copy(part, i, group):
            return send(
                following.at[part],
                following.at[part],
                weight_send.at[turn, i],
                weight_recv.at[turn, i],
                me,
                group,
            )

        def start_weight():
            return [weight_copy(g, 0, far), weight_copy(g, 1, mate)]

        weight_copies = start_weight()
        slope = gelu_slope(own_pre)
        plane = plane_in.at[turn, pl.ds(0, 15)]
        plane_all = whole(plane, plane, plane_send.at[turn], plane_recv.at[turn])
        plane_all.wait_recv()
        line_out[turn] = jnp.sum(plane_in[turn], axis=0)

        def send_line(k):
            tz = lax.rem(at_z + k + 1, 4)
            send(
                line_out.at[turn, tz],
                line_in.at[turn, at_z],
                line_send.at[turn],
                line_recv.at[turn],
                16 * at_y + 4 * tz + at_x,
                g,
            )

        each(3, send_line)
        line_in[turn, at_z] = line_out[turn, at_z]
        line = line_in.at[turn, pl.ds(0, 3)]
        line_all = whole(line, line, line_send.at[turn], line_recv.at[turn])
        line_all.wait_recv()

        hidden_grad = jnp.sum(line_in[turn], axis=0)
        pre_grad = (hidden_grad * slope).astype(BF16)
        parts = [part.astype(F32) for part in three_parts(pre_grad.astype(F32) * number)]
        in_grads = dot(jnp.concatenate(parts, axis=0).astype(BF16), code, 1, 0)
        in_grad = in_grads[0:8] + in_grads[8:16] + in_grads[16:24]
        row_weight, row_moment, row_second = adam_update(
            row_weight, row_moment, row_second, in_grad, step_count
        )
        if turn + 1 < ADAM:
            own_pre = dot(row_weight, code, 1, 1)
            hidden_own[...] = gelu_value(own_pre).astype(BF16)
            hidden_all[1, me] = hidden_own[...]
            source, target, several = hidden_own, hidden_all.at[1, me], hidden_all.at[1, most]
            send_sem, recv_sem = hidden_send, hidden_recv
        else:
            in_weight_new[core, me] = jnp.where(
                core == 0, row_weight[:, :256].astype(F32), row_weight[:, 256:].astype(F32)
            ).astype(BF16)
            source = target = in_weight_new.at[core, me]
            several = in_weight_new.at[core, most]
            send_sem, recv_sem = row_send, row_recv

        def send_rows(k):
            t = other(k)
            send(source, target, send_sem.at[0], recv_sem.at[0], t, g)

        each(others, send_rows)
        if turn + 1 == ADAM:
            in_moment_new[...] = row_moment
            in_second_new[...] = row_second
            out_moment_new[...] = moment
            out_second_new[...] = second_moment
        weight_copies[0].wait()
        weight_copies.append(weight_copy(far, 2, mate))
        whole(several, several, send_sem.at[0], recv_sem.at[0]).wait()
        if turn + 1 == ADAM:
            columns = in_weight_new.at[core]
            send(columns, columns, swap_send.at[0], swap_recv.at[0], me, mate).wait()
        for copy in weight_copies[1:]:
            copy.wait()
        plane_all.wait_send()
        line_all.wait_send()
        if turn + 1 < ADAM:
            current = following
            predict = dot(
                hidden_all[1].reshape(hidden_width, 128),
                current[...].reshape(hidden_width, 512),
                0,
                0,
            )
    own_all.wait_send()
    far_all.wait_send()

def store(*refs):
    sources, targets, sem = refs[:7], refs[7:14], refs[14]
    width = sources[1].shape[-1]
    pairs = [(sources[1].at[i], targets[1].at[:, :, pl.ds(width * i, width)]) for i in range(2)]
    pairs += [(sources[i], targets[i]) for i in (4, 5, 6, 0, 2, 3)]
    copies = [
        pltpu.make_async_copy(source, target, sem.at[i]) for i, (source, target) in enumerate(pairs)
    ]
    for copy in copies:
        copy.start()
    for copy in copies:
        copy.wait()

def shards(
    initial,
    react_rates,
    snap_times,
    field_code,
    time_code,
    batch_ids,
    in_weight,
    in_moment,
    in_second,
    out_weight,
    out_moment,
    out_second,
):
    strips = lax.axis_size("strip")
    fields_dev = initial.shape[0]
    hidden_width = in_weight.shape[0]
    points = out_weight.shape[1]
    vmem = pl.BlockSpec(memory_space=pltpu.VMEM)
    hbm = pl.BlockSpec(memory_space=pltpu.HBM)
    dma = pltpu.SemaphoreType.DMA
    outs = pl.pallas_call(
        kernel,
        out_shape=(
            pltpu.VMEM(initial.shape, F32),
            pltpu.VMEM((2, strips, 8, in_weight.shape[1] // 2), BF16),
            pltpu.VMEM(in_moment.shape, F32),
            pltpu.VMEM(in_second.shape, F32),
            pltpu.VMEM((4, hidden_width // 4, points), BF16),
            pltpu.VMEM(out_moment.shape, F32),
            pltpu.VMEM(out_second.shape, F32),
        ),
        in_specs=[hbm] * 12,
        out_specs=(vmem,) * 7,
        scratch_shapes=[
            pltpu.VMEM(initial.shape, F32),
            pltpu.SMEM(react_rates.shape, F32),
            pltpu.VMEM(snap_times.shape[::-1], jnp.int32),
            pltpu.VMEM(field_code.shape, BF16),
            pltpu.VMEM(time_code.shape, BF16),
            pltpu.VMEM(batch_ids.shape, jnp.int32),
            pltpu.VMEM((strips, 8, in_weight.shape[1]), BF16),
            pltpu.VMEM(in_moment.shape, F32),
            pltpu.VMEM(in_second.shape, F32),
            pltpu.VMEM((4, hidden_width // 4, points), BF16),
            pltpu.VMEM(out_moment.shape, F32),
            pltpu.VMEM(out_second.shape, F32),
            pltpu.VMEM((2, fields_dev, 2, 128), F32),
            pltpu.VMEM((2, fields_dev, 2, 128), F32),
            pltpu.VMEM((2 * fields_dev * 8, 128), F32),
            pltpu.VMEM((strips, 2, 128), BF16),
            pltpu.VMEM((4, strips, 2, 128), BF16),
            pltpu.VMEM((4, ADAM, 8, 128), F32),
            pltpu.VMEM((ADAM, 4, 4, 4, 8, 128), F32),
            pltpu.VMEM((ADAM, 16, 4, 8, 128), F32),
            pltpu.VMEM((ADAM, 4, 8, 128), F32),
            pltpu.VMEM((ADAM, 4, 8, 128), F32),
            pltpu.VMEM((8, 128), BF16),
            pltpu.VMEM((ADAM, strips, 8, 128), BF16),
            pltpu.VMEM((4, hidden_width // 4, points), BF16),
            dma((2,)),
            dma((2,)),
            dma((2,)),
            dma((1,)),
            dma((1,)),
            dma((1,)),
            dma((1,)),
            dma((3,)),
            dma((3,)),
            dma((ADAM,)),
            dma((ADAM,)),
            dma((ADAM,)),
            dma((ADAM,)),
            dma((1,)),
            dma((1,)),
            dma((ADAM, 3)),
            dma((ADAM, 3)),
            dma((1,)),
            dma((1,)),
            dma((12,)),
            dma((1,)),
            dma((1,)),
            pltpu.SemaphoreType.REGULAR,
        ],
        compiler_params=pltpu.CompilerParams(
            collective_id=0, has_side_effects=True, vmem_limit_bytes=48 * 1024 * 1024
        ),
        name="ensemble",
    )(
        *(
            pltpu.with_memory_space_constraint(operand, pltpu.HBM)
            for operand in (
        initial,
        react_rates,
        jnp.transpose(snap_times),
        field_code,
        time_code,
        batch_ids,
        in_weight.reshape(strips, hidden_width // strips, in_weight.shape[1]),
        in_moment,
        in_second,
        out_weight.reshape(4, hidden_width // 4, points),
        out_moment,
        out_second,
            )
        )
    )
    outs = pl.pallas_call(
        store,
        out_shape=tuple(
            pltpu.HBM((strips, 8, in_weight.shape[1]) if i == 1 else out.shape, out.dtype)
            for i, out in enumerate(outs)
        ),
        in_specs=[vmem] * 7,
        out_specs=(hbm,) * 7,
        scratch_shapes=[dma((8,))],
        name="store",
    )(*(pltpu.with_memory_space_constraint(out, pltpu.VMEM) for out in outs))
    fields, in_new, in_m, in_v, out_new, out_m, out_v = outs
    return (
        fields,
        in_new.reshape(in_weight.shape),
        in_m,
        in_v,
        out_new.reshape(out_weight.shape),
        out_m,
        out_v,
    )

def solution(mesh):
    in_specs = (
        P("group", "strip", None),
        P("group"),
        P(),
        P(),
        P(),
        P(None, "group"),
        P(),
        P("strip", None),
        P("strip", None),
        P(None, "strip"),
        P("group", "strip"),
        P("group", "strip"),
    )
    out_specs = (
        P("group", "strip", None),
        P(),
        P("strip", None),
        P("strip", None),
        P(None, "strip"),
        P("group", "strip"),
        P("group", "strip"),
    )
    return jax.shard_map(shards, mesh=mesh, in_specs=in_specs, out_specs=out_specs, check_vma=False)
```

```python
import functools

import jax
import jax.numpy as jnp
from jax import lax
from jax.experimental import pallas as pl
from jax.experimental.pallas import tpu as pltpu
from jax.sharding import PartitionSpec as P

STEPS = 2
SNAPS = 4
ADAM = 2
PRIOR = 100

DIFF_ROWS = 0.35
DIFF_COLS = 0.05
BETA_ONE = 0.9
BETA_TWO = 0.999
LEARN_RATE = 0.003
EPSILON = 1e-08
GELU_SCALE = 0.7978845608
GELU_CUBE = 0.044715

MESH = pl.DeviceIdType.MESH
F32 = jnp.float32
BF16 = jnp.bfloat16

def gelu_value(pre_act):
    return (
        0.5
        * pre_act
        * (1.0 + jnp.tanh(GELU_SCALE * (pre_act + GELU_CUBE * pre_act * pre_act * pre_act)))
    )

def gelu_slope(pre_act):
    tanh_part = jnp.tanh(GELU_SCALE * (pre_act + GELU_CUBE * pre_act * pre_act * pre_act))
    return 0.5 * (1.0 + tanh_part) + 0.5 * pre_act * (1.0 - tanh_part * tanh_part) * GELU_SCALE * (
        1.0 + 3.0 * GELU_CUBE * pre_act * pre_act
    )

def adam_update(weight, moment, second, gradient, step_count):
    moment = BETA_ONE * moment + (1.0 - BETA_ONE) * gradient
    second = BETA_TWO * second + (1.0 - BETA_TWO) * gradient * gradient
    update = (
        moment
        / (1.0 - BETA_ONE**step_count)
        / (jnp.sqrt(second / (1.0 - BETA_TWO**step_count)) + EPSILON)
    )
    return ((weight.astype(F32) - LEARN_RATE * update).astype(BF16), moment, second)

def dot(left, right, left_dim, right_dim):
    return lax.dot_general(
        left, right, (((left_dim,), (right_dim,)), ((), ())), preferred_element_type=F32
    )

def three_parts(value):
    high = value.astype(BF16)
    rest = value - high.astype(F32)
    middle = rest.astype(BF16)
    low = (rest - middle.astype(F32)).astype(BF16)
    return high, middle, low

def kernel(
    initial_hbm,
    rates_hbm,
    times_hbm,
    field_code_hbm,
    time_code_hbm,
    batch_ids_hbm,
    in_weight_hbm,
    in_moment_hbm,
    in_second_hbm,
    out_weight_hbm,
    out_moment_hbm,
    out_second_hbm,
    fields_out,
    in_weight_new,
    in_moment_new,
    in_second_new,
    out_weight_new,
    out_moment_new,
    out_second_new,
    initial,
    rates,
    times,
    field_code,
    time_code,
    batch_ids,
    in_weight,
    in_moment,
    in_second,
    out_weight,
    out_moment,
    out_second,
    edges,
    halo,
    states,
    pieces,
    arrived,
    counts,
    terms,
    plane_in,
    line_out,
    line_in,
    hidden_own,
    hidden_all,
    weight_mid,
    halo_send,
    halo_recv,
    piece_send,
    own_recv,
    far_recv,
    pool_send,
    pool_recv,
    count_send,
    count_recv,
    plane_send,
    plane_recv,
    line_send,
    line_recv,
    hidden_send,
    hidden_recv,
    weight_send,
    weight_recv,
    row_send,
    row_recv,
    load_sem,
    swap_send,
    swap_recv,
    plane_in_kernel,
):
    strips = lax.axis_size("strip")
    me = lax.axis_index("strip")
    g = lax.axis_index("group")
    far = lax.rem(g + 2, 4)
    mate = g + 1 - 2 * lax.rem(g, 2)
    far_mate = lax.rem(mate + 2, 4)
    fields = initial.shape[0]
    others = strips - 1
    core = lax.rem(g, 2)
    at_y, at_z, at_x = me // 16, lax.rem(me // 4, 4), lax.rem(me, 4)

    def each(count, body):
        width = next(w for w in (21, 15, 3) if count % w == 0)

        def steps(k, carry):
            for i in range(width):
                body(width * k + i)
            return carry

        lax.fori_loop(0, count // width, steps, 0)

    def other(k):
        return lax.rem(me + 1 + k, strips)

    def send(source, target, send_sem, recv_sem, strip, group):
        copy = pltpu.make_async_remote_copy(
            src_ref=source,
            dst_ref=target,
            send_sem=send_sem,
            recv_sem=recv_sem,
            device_id={"strip": strip, "group": group},
            device_id_type=MESH,
        )
        copy.start()
        return copy

    loads = [
        pltpu.make_async_copy(source, target, load_sem.at[i])
        for i, (source, target) in enumerate(
            (
                (initial_hbm, initial),
                (batch_ids_hbm, batch_ids),
                (times_hbm, times),
                (field_code_hbm, field_code),
                (time_code_hbm, time_code),
                (in_weight_hbm, in_weight),
                (rates_hbm, rates),
                (out_weight_hbm, out_weight),
                (in_moment_hbm, in_moment),
                (in_second_hbm, in_second),
                (out_moment_hbm, out_moment),
                (out_second_hbm, out_second),
            )
        )
    ]
    for load in loads:
        load.start()

    barrier = pltpu.get_barrier_semaphore()

    def greet(strip, group):
        pl.semaphore_signal(
            barrier, inc=1, device_id={"strip": strip, "group": group}, device_id_type=MESH
        )

    plane_peers = []
    line_peers = []
    for i in range(1, 16):
        ty, tx = lax.rem(at_y + i // 4, 4), lax.rem(at_x + i % 4, 4)
        plane_peers.append((16 * ty + 4 * at_z + tx, g))
    for i in range(1, 4):
        strip = 16 * at_y + 4 * lax.rem(at_z + i, 4) + at_x
        line_peers += [(strip, far), (strip, g)]
    line_peers.append((me, far))
    up = lax.rem(me + others, strips)
    down = lax.rem(me + 1, strips)
    for strip, group in [(up, g), (down, g)] + line_peers + plane_peers + [(me, mate), (me, far_mate)]:
        greet(strip, group)
    greeted = 26

    loads[0].wait()
    edges[0] = initial[:, 0:2, :]
    edges[1] = initial[:, 2:4, :]

    pl.semaphore_wait(barrier, greeted)

    halo_copies = [
        send(edges.at[0], halo.at[1], halo_send.at[0], halo_recv.at[1], up, g),
        send(edges.at[1], halo.at[0], halo_send.at[1], halo_recv.at[0], down, g),
    ]
    for strip, group in line_peers:
        pl.semaphore_signal(
            plane_in_kernel,
            inc=1,
            device_id={"strip": strip, "group": group},
            device_id_type=MESH,
        )
    for load in loads[1:3]:
        load.wait()
    kind_row = lax.broadcasted_iota(jnp.int32, (128, 128), 0)
    field_row = 16 * (kind_row // 32) + lax.rem(kind_row, 16)
    kind_lane = lax.broadcasted_iota(jnp.int32, (64, 128), 1)
    field_lane = 16 * (kind_lane // 32) + lax.rem(kind_lane, 16)
    spread = (lax.broadcasted_iota(jnp.int32, (64, 128), 0) == field_lane).astype(F32).astype(BF16)
    kind_times = dot(times[...].astype(F32).astype(BF16), spread, 1, 0)
    slot = lax.broadcasted_iota(jnp.int32, (4, 128), 0)
    own_time = jnp.sum(jnp.where(slot == g, kind_times, 0.0), axis=0, keepdims=True)
    step_lane = (lax.rem(lax.broadcasted_iota(jnp.int32, (1, 128), 1) // 16, 2) + 1).astype(F32)
    time_fits = jnp.where(own_time == step_lane, 1.0, 0.0)
    ones = jnp.ones((8, 128), BF16)
    for turn in range(ADAM):
        hits = (batch_ids[turn : turn + 1, :] == field_row).astype(F32).astype(BF16)
        counts[0, turn] = dot(ones, hits, 1, 1) * time_fits

    count_copies = [
        send(counts.at[0], counts.at[1 + i], count_send.at[i], count_recv.at[i], me, group)
        for i, group in enumerate((far, mate, far_mate))
    ]

    for load in loads[6:]:
        load.wait()

    for load in loads[3:6]:
        load.wait()
    code_parts = []
    for part in range(4):
        for step in range(STEPS):
            code_parts.append(
                (
                    field_code[16 * part : 16 * part + 16, :].astype(F32)
                    + time_code[step : step + 1, :].astype(F32)
                ).astype(BF16)
            )
    code = jnp.concatenate(code_parts, axis=0)
    hidden_width = 8 * strips
    pre_act = dot(in_weight[...].reshape(hidden_width, 512), code, 1, 1)
    hidden = gelu_value(pre_act).astype(BF16)
    hidden_all[0] = hidden.reshape(strips, 8, 128)

    old_weight = out_weight[...].reshape(hidden_width, 512)
    predict = dot(hidden, old_weight, 0, 0)
    own_pre = dot(in_weight[me], code, 1, 1)

    for copy in halo_copies:
        copy.wait()

    row = lax.broadcasted_iota(jnp.int32, (8, 128), 0) + 4 * me - 2
    inside = jnp.logical_and(row >= 0, row < 4 * strips)

    def advance(center, rate):
        across = pltpu.roll(center, 1, 1) + pltpu.roll(center, 127, 1)
        return (
            center
            + DIFF_ROWS * (pltpu.roll(center, 1, 0) + pltpu.roll(center, 7, 0) - 2.0 * center)
            + DIFF_COLS * (across - 2.0 * center)
            + rate * center * (1.0 - center * center)
        )

    for field in range(fields):
        start = jnp.concatenate([halo[0, field], initial[field], halo[1, field]], axis=0)
        start = jnp.where(inside, start, 0.0)
        first = jnp.where(inside, advance(start, rates[field]), 0.0)
        second = advance(first, rates[field])
        states[8 * field : 8 * field + 8, :] = first
        states[8 * (fields + field) : 8 * (fields + field) + 8, :] = second
        fields_out[field] = second[2:6, :]

    def grid(shape):
        return (lax.broadcasted_iota(jnp.int32, shape, i) for i in range(2))

    def one_hot(hit):
        return jnp.where(hit, 1.0, 0.0).astype(BF16)

    kind_at, lane_at = grid((32, 128))
    repeat = one_hot(kind_at == lax.rem(lane_at, 32))
    point_at, lane_at = grid((128, 128))
    own_lanes = lax.rem(point_at, 4) == lane_at // 32
    four_at, point_at = grid((32, 128))
    fold = one_hot(four_at == point_at // 4)
    for line in range(4):
        chosen = states[pl.ds(2 + line, 32, stride=8), :].astype(BF16)
        spread_out = jnp.where(own_lanes, dot(chosen, repeat, 0, 0), 0.0).astype(BF16)
        piece = dot(fold, spread_out, 1, 0)
        pieces[16 * line : 16 * line + 16] = piece.reshape(16, 2, 128).astype(BF16)

    pl.semaphore_wait(plane_in_kernel, 7)
    def send_piece(k):
        t = other(k)
        send(pieces.at[t], arrived.at[0, me], piece_send.at[0], own_recv.at[0], t, g)
        send(pieces.at[t], arrived.at[1, me], piece_send.at[1], far_recv.at[0], t, far)

    each(others, send_piece)
    send(pieces.at[me], arrived.at[1, me], piece_send.at[1], far_recv.at[0], me, far)
    arrived[0, me] = pieces[me]

    def whole(source, target, send_sem, recv_sem):
        return pltpu.make_async_remote_copy(
            src_ref=source,
            dst_ref=target,
            send_sem=send_sem,
            recv_sem=recv_sem,
            device_id={"strip": me, "group": far},
            device_id_type=MESH,
        )

    most = pl.ds(0, others)
    own_all = whole(pieces.at[most], arrived.at[0, most], piece_send.at[0], own_recv.at[0])
    far_all = whole(pieces, arrived.at[1], piece_send.at[1], far_recv.at[0])
    own_all.wait_recv()
    far_all.wait_recv()
    pool_copy = send(
        arrived.at[pl.ds(0, 2)], arrived.at[pl.ds(2, 2)], pool_send.at[0], pool_recv.at[0], me, mate
    )
    for copy in count_copies:
        copy.wait()
    count = jnp.sum(counts[...], axis=0)
    point_at, row_at = grid((8 * strips, 2 * strips))
    unfold = one_hot(point_at // 4 == row_at)
    point_at, lane_at = grid((8 * strips, 128))
    lane_at2 = lax.broadcasted_iota(jnp.int32, (8 * strips, 256), 1)
    own_lanes = lax.rem(lax.broadcasted_iota(jnp.int32, (8 * strips, 256), 0), 4) == (
        lax.rem(lane_at2, 128) // 32
    )
    lane_at, kind_at = grid((256, 128))

    def pool_of(part, group, other_group):
        rows = [
            arrived[part + i].astype(F32).reshape(2 * strips, 128).astype(BF16) for i in range(2)
        ]
        points = dot(unfold, jnp.concatenate(rows, axis=1), 1, 0)
        points = jnp.where(own_lanes, points, 0.0).astype(BF16)
        start = jnp.where(lane_at < 128, 32 * group, 32 * other_group)
        return dot(one_hot(kind_at == start + lax.rem(lane_at, 32)), points, 0, 1)

    pool = pool_of(0, g, far)
    pool_copy.wait()
    pool = pool + pool_of(2, mate, far_mate)

    moment, second_moment = out_moment[...], out_second[...]
    row_weight, row_moment, row_second = in_weight[me], in_moment[...], in_second[...]
    current = out_weight
    for turn in range(ADAM):
        step_count = PRIOR + turn + 1
        number = count[turn, 0:1, :]
        delta = ((predict - pool) * (1.0 / 512.0)).astype(BF16)
        weights = current[...].reshape(hidden_width, 512)

        terms[turn] = dot(weights, delta, 1, 1).reshape(4, 4, 4, 8, 128)

        def send_terms(k):
            ty = lax.rem(at_y + (k + 1) // 4, 4)
            tx = lax.rem(at_x + lax.rem(k + 1, 4), 4)
            send(
                terms.at[turn, ty, :, tx],
                plane_in.at[turn, 4 * at_y + at_x],
                plane_send.at[turn],
                plane_recv.at[turn],
                16 * ty + 4 * at_z + tx,
                g,
            )

        each(15, send_terms)
        plane_in[turn, 4 * at_y + at_x] = terms[turn, at_y, :, at_x]

        own_hidden = hidden_all[turn, pl.ds(g * (strips // 4), strips // 4)].reshape(
            hidden_width // 4, 128
        )
        grad = sum(dot(part, delta, 1, 0) for part in three_parts(own_hidden.astype(F32) * number))
        new_rows, moment, second_moment = adam_update(
            current[g], moment, second_moment, grad, step_count
        )
        following = weight_mid if turn + 1 < ADAM else out_weight_new
        following[g] = new_rows

        def weight_copy(part, i, group):
            return send(
                following.at[part],
                following.at[part],
                weight_send.at[turn, i],
                weight_recv.at[turn, i],
                me,
                group,
            )

        def start_weight():
            return [weight_copy(g, 0, far), weight_copy(g, 1, mate)]

        weight_copies = start_weight()
        slope = gelu_slope(own_pre)
        plane = plane_in.at[turn, pl.ds(0, 15)]
        plane_all = whole(plane, plane, plane_send.at[turn], plane_recv.at[turn])
        plane_all.wait_recv()
        line_out[turn] = jnp.sum(plane_in[turn], axis=0)

        def send_line(k):
            tz = lax.rem(at_z + k + 1, 4)
            send(
                line_out.at[turn, tz],
                line_in.at[turn, at_z],
                line_send.at[turn],
                line_recv.at[turn],
                16 * at_y + 4 * tz + at_x,
                g,
            )

        each(3, send_line)
        line_in[turn, at_z] = line_out[turn, at_z]
        line = line_in.at[turn, pl.ds(0, 3)]
        line_all = whole(line, line, line_send.at[turn], line_recv.at[turn])
        line_all.wait_recv()

        hidden_grad = jnp.sum(line_in[turn], axis=0)
        pre_grad = (hidden_grad * slope).astype(BF16)
        parts = [part.astype(F32) for part in three_parts(pre_grad.astype(F32) * number)]
        in_grads = dot(jnp.concatenate(parts, axis=0).astype(BF16), code, 1, 0)
        in_grad = in_grads[0:8] + in_grads[8:16] + in_grads[16:24]
        row_weight, row_moment, row_second = adam_update(
            row_weight, row_moment, row_second, in_grad, step_count
        )
        if turn + 1 < ADAM:
            own_pre = dot(row_weight, code, 1, 1)
            hidden_own[...] = gelu_value(own_pre).astype(BF16)
            hidden_all[1, me] = hidden_own[...]
            source, target, several = hidden_own, hidden_all.at[1, me], hidden_all.at[1, most]
            send_sem, recv_sem = hidden_send, hidden_recv
        else:
            in_weight_new[core, me] = jnp.where(
                core == 0, row_weight[:, :256].astype(F32), row_weight[:, 256:].astype(F32)
            ).astype(BF16)
            source = target = in_weight_new.at[core, me]
            several = in_weight_new.at[core, most]
            send_sem, recv_sem = row_send, row_recv

        def send_rows(k):
            t = other(k)
            send(source, target, send_sem.at[0], recv_sem.at[0], t, g)

        each(others, send_rows)
        if turn + 1 == ADAM:
            in_moment_new[...] = row_moment
            in_second_new[...] = row_second
            out_moment_new[...] = moment
            out_second_new[...] = second_moment
        weight_copies[0].wait()
        weight_copies.append(weight_copy(far, 2, mate))
        whole(several, several, send_sem.at[0], recv_sem.at[0]).wait()
        if turn + 1 == ADAM:
            columns = in_weight_new.at[core]
            send(columns, columns, swap_send.at[0], swap_recv.at[0], me, mate).wait()
        for copy in weight_copies[1:]:
            copy.wait()
        plane_all.wait_send()
        line_all.wait_send()
        if turn + 1 < ADAM:
            current = following
            predict = dot(
                hidden_all[1].reshape(hidden_width, 128),
                current[...].reshape(hidden_width, 512),
                0,
                0,
            )
    own_all.wait_send()
    far_all.wait_send()

def store(*refs):
    sources, targets, sem = refs[:7], refs[7:14], refs[14]
    width = sources[1].shape[-1]
    pairs = [(sources[1].at[i], targets[1].at[:, :, pl.ds(width * i, width)]) for i in range(2)]
    pairs += [(sources[i], targets[i]) for i in (4, 5, 6, 0, 2, 3)]
    copies = [
        pltpu.make_async_copy(source, target, sem.at[i]) for i, (source, target) in enumerate(pairs)
    ]
    for copy in copies:
        copy.start()
    for copy in copies:
        copy.wait()

def shards(
    initial,
    react_rates,
    snap_times,
    field_code,
    time_code,
    batch_ids,
    in_weight,
    in_moment,
    in_second,
    out_weight,
    out_moment,
    out_second,
):
    strips = lax.axis_size("strip")
    fields_dev = initial.shape[0]
    hidden_width = in_weight.shape[0]
    points = out_weight.shape[1]
    vmem = pl.BlockSpec(memory_space=pltpu.VMEM)
    hbm = pl.BlockSpec(memory_space=pltpu.HBM)
    dma = pltpu.SemaphoreType.DMA
    outs = pl.pallas_call(
        kernel,
        out_shape=(
            pltpu.VMEM(initial.shape, F32),
            pltpu.VMEM((2, strips, 8, in_weight.shape[1] // 2), BF16),
            pltpu.VMEM(in_moment.shape, F32),
            pltpu.VMEM(in_second.shape, F32),
            pltpu.VMEM((4, hidden_width // 4, points), BF16),
            pltpu.VMEM(out_moment.shape, F32),
            pltpu.VMEM(out_second.shape, F32),
        ),
        in_specs=[hbm] * 12,
        out_specs=(vmem,) * 7,
        scratch_shapes=[
            pltpu.VMEM(initial.shape, F32),
            pltpu.SMEM(react_rates.shape, F32),
            pltpu.VMEM(snap_times.shape[::-1], jnp.int32),
            pltpu.VMEM(field_code.shape, BF16),
            pltpu.VMEM(time_code.shape, BF16),
            pltpu.VMEM(batch_ids.shape, jnp.int32),
            pltpu.VMEM((strips, 8, in_weight.shape[1]), BF16),
            pltpu.VMEM(in_moment.shape, F32),
            pltpu.VMEM(in_second.shape, F32),
            pltpu.VMEM((4, hidden_width // 4, points), BF16),
            pltpu.VMEM(out_moment.shape, F32),
            pltpu.VMEM(out_second.shape, F32),
            pltpu.VMEM((2, fields_dev, 2, 128), F32),
            pltpu.VMEM((2, fields_dev, 2, 128), F32),
            pltpu.VMEM((2 * fields_dev * 8, 128), F32),
            pltpu.VMEM((strips, 2, 128), BF16),
            pltpu.VMEM((4, strips, 2, 128), BF16),
            pltpu.VMEM((4, ADAM, 8, 128), F32),
            pltpu.VMEM((ADAM, 4, 4, 4, 8, 128), F32),
            pltpu.VMEM((ADAM, 16, 4, 8, 128), F32),
            pltpu.VMEM((ADAM, 4, 8, 128), F32),
            pltpu.VMEM((ADAM, 4, 8, 128), F32),
            pltpu.VMEM((8, 128), BF16),
            pltpu.VMEM((ADAM, strips, 8, 128), BF16),
            pltpu.VMEM((4, hidden_width // 4, points), BF16),
            dma((2,)),
            dma((2,)),
            dma((2,)),
            dma((1,)),
            dma((1,)),
            dma((1,)),
            dma((1,)),
            dma((3,)),
            dma((3,)),
            dma((ADAM,)),
            dma((ADAM,)),
            dma((ADAM,)),
            dma((ADAM,)),
            dma((1,)),
            dma((1,)),
            dma((ADAM, 3)),
            dma((ADAM, 3)),
            dma((1,)),
            dma((1,)),
            dma((12,)),
            dma((1,)),
            dma((1,)),
            pltpu.SemaphoreType.REGULAR,
        ],
        compiler_params=pltpu.CompilerParams(
            collective_id=0, has_side_effects=True, vmem_limit_bytes=48 * 1024 * 1024
        ),
        name="ensemble",
    )(
        *(
            pltpu.with_memory_space_constraint(operand, pltpu.HBM)
            for operand in (
        initial,
        react_rates,
        jnp.transpose(snap_times),
        field_code,
        time_code,
        batch_ids,
        in_weight.reshape(strips, hidden_width // strips, in_weight.shape[1]),
        in_moment,
        in_second,
        out_weight.reshape(4, hidden_width // 4, points),
        out_moment,
        out_second,
            )
        )
    )
    outs = pl.pallas_call(
        store,
        out_shape=tuple(
            pltpu.HBM((strips, 8, in_weight.shape[1]) if i == 1 else out.shape, out.dtype)
            for i, out in enumerate(outs)
        ),
        in_specs=[vmem] * 7,
        out_specs=(hbm,) * 7,
        scratch_shapes=[dma((8,))],
        name="store",
    )(*(pltpu.with_memory_space_constraint(out, pltpu.VMEM) for out in outs))
    fields, in_new, in_m, in_v, out_new, out_m, out_v = outs
    return (
        fields,
        in_new.reshape(in_weight.shape),
        in_m,
        in_v,
        out_new.reshape(out_weight.shape),
        out_m,
        out_v,
    )

def solution(mesh):
    in_specs = (
        P("group", "strip", None),
        P("group"),
        P(),
        P(),
        P(),
        P(None, "group"),
        P(),
        P("strip", None),
        P("strip", None),
        P(None, "strip"),
        P("group", "strip"),
        P("group", "strip"),
    )
    out_specs = (
        P("group", "strip", None),
        P(),
        P("strip", None),
        P("strip", None),
        P(None, "strip"),
        P("group", "strip"),
        P("group", "strip"),
    )
    return jax.shard_map(shards, mesh=mesh, in_specs=in_specs, out_specs=out_specs, check_vma=False)
```
